512 devices in a mesh: grp: 8 (over y), sub: 64 (over x, z, core).
Axes of the slice: x: 4, y: 8, z: 8, core: 2. Of those that a mesh axis runs over, the one named last changes fastest.
Arguments:
- omega: bfloat16 [393216, 256], P(('grp', 'sub')), may hold values from -6 to 6
- adj_tests: bfloat16 [256, 393216], P('sub', 'grp'), may hold values from -6 to 6
- near_tiles: bfloat16 [3072, 12, 128, 128], P(('grp', 'sub')), may hold values from -0.15625 to 0.15625
- tile_cols: int32 [3072, 12], P(('grp', 'sub')), may hold values from 0 to 3071, as said below
- leaf_perms: int32 [512, 2, 768], P(('grp', 'sub')), may hold values from 0 to 767, each once within a row
- leaf_interp: bfloat16 [512, 2, 672, 96], P(('grp', 'sub')), may hold values from -0.125 to 0.125
- node_perms: int32 [512, 9, 2, 192], P(('grp', 'sub')), may hold values from 0 to 191, as said below
- node_maps: bfloat16 [512, 9, 4, 96, 96], P(('grp', 'sub')), as said below
Outputs:
- path_panels: bfloat16 [512, 9, 2, 96, 256], P(('grp', 'sub'))
The draws below stay inside these ranges and needn't reach their ends.
Inputs may be any that keep to these rules, and one draw needn't show every extreme that they name: `tile_cols`: the 12 column tiles of tile row q are distinct and lie in the tile rows of its own leaf or of the leaves just before and after it within the same block of 64 leaves; each block of 64 leaves is one index of grp. `leaf_perms`: each of the two orders of a leaf is a permutation of 0 to 767. `node_perms`: each order is a permutation of 0 to 191; entries [d, j] are equal for all d with the same d // 2^(j+1). `node_maps`: entries [d, j] are equal for all d with the same d // 2^(j+1).
All inputs are finite; a program needn't handle non-finite values.
Results may differ from the reference program's by a relative error of at most 0.0065.
Values may be sent and summed in bfloat16 or wider, within the bound.
A program may use at most 64 MiB of HBM per device.

```python
import math
import jax
import jax.numpy as jnp
from jax import lax

M = 768
TILE = 128
NT = 12
S = 256
K = 96
LEAVES = 512
NROWS = 393216
NROWT = 3072
LEVX = 9
N_SUB = 64


def node_owner():
    return jnp.right_shift(jnp.arange(LEAVES, dtype=jnp.int32)[:, None], jnp.arange(LEVX, dtype=jnp.int32)[None, :] + 1)


def draw_tile_cols(key, part):
    per_dev = M // TILE
    span = 3 * per_dev
    rows = jnp.arange(NROWT, dtype=jnp.int32)
    device = rows // per_dev
    place = device % N_SUB
    slots = jnp.arange(span, dtype=jnp.int32)[None, :]
    valid = ((slots >= per_dev) | (place[:, None] > 0)) & ((slots < 2 * per_dev) | (place[:, None] < N_SUB - 1))
    scores = jax.random.randint(key, (NROWT, span), 0, 1 << 20, dtype=jnp.int32)
    ranked = scores * span + slots + jnp.where(valid, 0, 1 << 29)
    chosen = jnp.argsort(ranked, axis=1, stable=True)[:, :NT].astype(jnp.int32)
    return ((device[:, None] - 1) * per_dev + chosen).astype(jnp.int32)


def draw_node_perms(key, part):
    nodes = LEAVES // 2
    keys = jax.random.split(key, LEVX * nodes * 2)
    full = jax.vmap(lambda k: jax.random.permutation(k, 2 * K))(keys).reshape(LEVX, nodes, 2, 2 * K)
    return full[jnp.arange(LEVX, dtype=jnp.int32)[None, :], node_owner()].astype(jnp.int32)


def draw_node_maps(key, part):
    nodes = LEAVES // 2
    full = jax.random.normal(key, (LEVX, nodes, 4, K, K), jnp.float32)
    scales = jnp.array([0.35, 0.35, 0.5, 0.5], jnp.float32)[:, None, None] / math.sqrt(K)
    full = full * scales
    return full[jnp.arange(LEVX, dtype=jnp.int32)[None, :], node_owner()].astype(jnp.bfloat16)


def shard_levels(key, extent, cuts, low, largest):
    factor_of, own = 1.0, jax.random.fold_in(key, 6)
    for axis_at, parts in cuts:
        steps = jnp.exp(jax.random.uniform(jax.random.fold_in(own, axis_at), (parts,), jnp.float32, low / len(cuts), largest / len(cuts)))
        factor_of = factor_of * jnp.repeat(steps, extent[axis_at] // parts).reshape([-1 if axis == axis_at else 1 for axis in range(len(extent))])
    return factor_of


def centred(own_key, shape, scale, most, cuts=(), kind=jnp.bfloat16):
    values = jax.random.normal(own_key, shape, jnp.float32) * scale
    if len(cuts) > 0:
        values = shard_levels(own_key, shape, cuts, -0.22, 0.18) * values
    return jnp.clip(values, min=-most, max=most).astype(kind)


def setup_inputs(seed: int = 0) -> dict:
    arg_keys = jax.random.split(jax.random.key(seed), 9)
    return {
        "omega": centred(arg_keys[0], (NROWS, S), 1.0, 6.0, ((0, 512),)),
        "adj_tests": centred(arg_keys[1], (S, NROWS), 1.0, 6.0, ((0, 64), (1, 8))),
        "near_tiles": centred(arg_keys[2], (NROWT, NT, TILE, TILE), (NT * TILE) ** -0.5, 0.15625, ((0, 512),)),
        "tile_cols": draw_tile_cols(jax.random.fold_in(arg_keys[8], 71), 0),
        "leaf_perms": jax.vmap(lambda own: jax.random.permutation(own, M))(jax.random.split(arg_keys[4], LEAVES * 2)).reshape((LEAVES, 2, M)).astype(jnp.int32),
        "leaf_interp": centred(arg_keys[5], (LEAVES, 2, M - K, K), (4 * (M - K)) ** -0.5, 0.125, ((0, 512),)),
        "node_perms": draw_node_perms(jax.random.fold_in(arg_keys[8], 71), 0),
        "node_maps": draw_node_maps(jax.random.fold_in(arg_keys[8], 71), 0),
    }


HIGHEST = lax.Precision.HIGHEST


def apply_rows(matrix, panel):
    return jnp.einsum("...ij,...js->...is", matrix, panel, precision=HIGHEST)


def apply_cols(matrix, panel):
    return jnp.einsum("...ji,...js->...is", matrix, panel, precision=HIGHEST)


def pick_rows(panel, order):
    return jnp.take_along_axis(panel, order[..., None], axis=-2)


def squeeze_node(fwd_rows, fwd_tests, adj_rows, adj_panel, row_order, col_order, row_interp, col_interp):
    rank = row_interp.shape[-1]
    fwd_skel = pick_rows(fwd_rows, row_order[..., :rank])
    test_skel = pick_rows(fwd_tests, col_order[..., :rank]) + apply_cols(col_interp, pick_rows(fwd_tests, col_order[..., rank:]))
    adj_skel = pick_rows(adj_rows, col_order[..., :rank])
    adj_test_skel = pick_rows(adj_panel, row_order[..., :rank]) + apply_cols(row_interp, pick_rows(adj_panel, row_order[..., rank:]))
    return fwd_skel, test_skel, adj_skel, adj_test_skel


def merge_pair(lower, upper, maps, orders):
    maps = maps.astype(jnp.float32)
    row_interp = maps[..., 0, :, :]
    col_interp = maps[..., 1, :, :]
    low_high = maps[..., 2, :, :]
    high_low = maps[..., 3, :, :]
    fwd_rows = jnp.concatenate([lower[0] - apply_rows(low_high, upper[1]), upper[0] - apply_rows(high_low, lower[1])], axis=-2)
    fwd_tests = jnp.concatenate([lower[1], upper[1]], axis=-2)
    adj_rows = jnp.concatenate([lower[2] - apply_cols(high_low, upper[3]), upper[2] - apply_cols(low_high, lower[3])], axis=-2)
    adj_panel = jnp.concatenate([lower[3], upper[3]], axis=-2)
    return squeeze_node(fwd_rows, fwd_tests, adj_rows, adj_panel, orders[..., 0, :], orders[..., 1, :], row_interp, col_interp)


def reference(omega, adj_tests, near_tiles, tile_cols, leaf_perms, leaf_interp, node_perms, node_maps):
    per_dev = M // TILE
    omega_tiles = omega.reshape(NROWT, TILE, S)
    tiles_dev = near_tiles.reshape(LEAVES, per_dev, NT, TILE, TILE)
    cols_dev = tile_cols.reshape(LEAVES, per_dev, NT)

    def forward_one(inputs):
        tiles, cols = inputs
        picked = omega_tiles[cols].astype(jnp.float32)
        return jnp.einsum("rtij,rtjs->ris", tiles.astype(jnp.float32), picked, precision=HIGHEST).reshape(M, S)

    forward = lax.map(forward_one, (tiles_dev, cols_dev))
    adj_dev = adj_tests.reshape(S, LEAVES, per_dev, TILE).transpose(1, 0, 2, 3)

    def adjoint_one(total, inputs):
        tiles, cols, tests = inputs
        contrib = jnp.einsum("rtij,sri->rtjs", tiles.astype(jnp.float32), tests.astype(jnp.float32), precision=HIGHEST)
        return total.at[cols].add(contrib), None

    adjoint, _ = lax.scan(adjoint_one, jnp.zeros((NROWT, TILE, S), jnp.float32), (tiles_dev, cols_dev, adj_dev))
    adjoint = adjoint.reshape(LEAVES, M, S)
    omega_leaf = omega.reshape(LEAVES, M, S).astype(jnp.float32)
    adj_leaf = adj_tests.reshape(S, LEAVES, M).transpose(1, 2, 0).astype(jnp.float32)
    interp = leaf_interp.astype(jnp.float32)
    panels = squeeze_node(forward, omega_leaf, adjoint, adj_leaf, leaf_perms[:, 0], leaf_perms[:, 1], interp[:, 0], interp[:, 1])
    levels = []
    for level in range(LEVX):
        stride = 2 ** (level + 1)
        lower = tuple(x[0::2] for x in panels)
        upper = tuple(x[1::2] for x in panels)
        panels = merge_pair(lower, upper, node_maps[::stride, level], node_perms[::stride, level])
        levels.append(jnp.repeat(jnp.stack([panels[0], panels[2]], axis=1), stride, axis=0))
    return jnp.stack(levels, axis=1).astype(jnp.bfloat16)
```

```python
import jax
import jax.numpy as jnp
from jax import lax
from jax.experimental import pallas as pl
from jax.experimental.pallas import tpu as pltpu
from jax.sharding import PartitionSpec as P

BF = jnp.bfloat16
F32 = jnp.float32
MESH = pl.DeviceIdType.MESH
K = 96
LEVELS = 9


def mm(a, b):
    return lax.dot_general(a, b, (((1,), (0,)), ((), ())), preferred_element_type=F32)


def mm_nt(a, b):
    return lax.dot_general(a, b, (((1,), (1,)), ((), ())), preferred_element_type=F32)


def mm_tn(a, b):
    return lax.dot_general(a, b, (((0,), (0,)), ((), ())), preferred_element_type=F32)


def onehot(column, width):
    lanes = lax.broadcasted_iota(jnp.int32, (column.shape[0], width), 1)
    return jnp.where(lanes == column, 1.0, 0.0)


def build_kernel(inv, heads, tails, node_cols, near, interp, maps, wf, wa, gl, op_s, op_h, op_g, placed):
    def place(q, carry):
        for m in range(18):
            t = inv[q, m]
            tile = near[q * 12 + jnp.maximum(t - 1, 0)]
            keep = jnp.where(t > 0, 1.0, 0.0)
            placed[pl.ds(pl.multiple_of(q * 128, 128), 128), m * 128 : (m + 1) * 128] = tile * keep.astype(BF)
        return carry

    lax.fori_loop(0, 6, place, 0)
    wf[...] = mm(onehot(heads[:, 0:1], 768).astype(BF), placed[...]).astype(BF)
    for k, col in enumerate((2, 1, 3)):
        pick = onehot(heads[:, col : col + 1], 768).astype(BF)
        wa[k] = mm_nt(pick, placed[:, k * 768 : (k + 1) * 768]).astype(BF)
    for i in range(2):
        tail = onehot(tails[:, i : i + 1], 768).astype(BF)
        gl[i] = (onehot(heads[:, i : i + 1], 768) + mm_tn(interp[i], tail)).astype(BF)

    def level(j, carry):
        picks = [onehot(node_cols[j][:, i : i + 1], 256) for i in range(2)]
        low_high, high_low = maps[j * 4 + 2], maps[j * 4 + 3]
        for ch in range(2):
            sel = picks[ch][:K].astype(BF)
            tests = picks[1 - ch]
            full = (tests[:K] + mm_tn(maps[j * 4 + 1 - ch], tests[K:].astype(BF))).astype(BF)
            couple = (high_low, low_high) if ch == 0 else (low_high, high_low)
            times = mm if ch == 0 else mm_nt
            for half in range(2):
                at = (j * 2 + ch) * 2 + half
                op_s[at] = sel[:, half * 128 : half * 128 + 128]
                op_g[at] = full[:, half * 128 : half * 128 + 128]
                other = sel[:, (1 - half) * 128 : (1 - half) * 128 + K]
                op_h[at, :, 0:K] = times(other, couple[half]).astype(BF)
        return carry

    lax.fori_loop(0, LEVELS, level, 0)


def vmem():
    return pl.BlockSpec(memory_space=pltpu.VMEM)


def build(inv, heads, tails, node_cols, near, interp, maps):
    ops = jax.ShapeDtypeStruct((LEVELS * 4, K, 128), BF)
    return pl.pallas_call(
        build_kernel,
        out_shape=(
            jax.ShapeDtypeStruct((K, 2304), BF),
            jax.ShapeDtypeStruct((3, K, 768), BF),
            jax.ShapeDtypeStruct((2, K, 768), BF),
            ops,
            ops,
            ops,
        ),
        in_specs=[pl.BlockSpec(memory_space=pltpu.SMEM)] + [vmem()] * 6,
        out_specs=tuple(vmem() for _ in range(6)),
        scratch_shapes=[pltpu.VMEM((768, 2304), BF)],
        compiler_params=pltpu.CompilerParams(vmem_limit_bytes=48 << 20),
        cost_estimate=pl.CostEstimate(flops=2_000_000_000, bytes_accessed=8_000_000, transcendentals=0),
        name="build",
    )(inv, heads, tails, node_cols, near, interp, maps)


def mirror(z):
    return lax.rem(jnp.where(lax.rem(z, 2) == 0, 14 - z, 16 - z), 8)


def tree_kernel(
    om_low, om, om_high, adj, wf, wa, gl, op_s, op_h, op_g,
    out, pan, halo_s, halo_r, s0, r0, hi, lo, rec,
    halo_ss, halo_rs, ss0, rs0, ss, rs, os_s, os_r,
):
    g = lax.axis_index("grp")
    s = lax.axis_index("sub")
    core = lax.rem(s, 2)
    z = lax.rem(s // 2, 8)
    x = s // 16
    z0 = lax.rem(z, 2)
    left, right = lax.rem(s + 63, 64), lax.rem(s + 1, 64)

    def sub_at(xx, zz, cc):
        return (xx * 8 + zz) * 2 + cc

    def flip(v, bit):
        return jnp.where(lax.rem(v // bit, 2) == 0, v + bit, v - bit)

    mate = sub_at(x, z, 1 - core)
    zmate = sub_at(x, flip(z, 1), core)
    cross = sub_at(x, flip(z, 1), 1 - core)
    partners = [
        {"sub": mate},
        {"sub": zmate},
        {"sub": sub_at(x, flip(z, 2), core)},
        {"sub": sub_at(x, mirror(z), core)},
        {"sub": sub_at(flip(x, 1), z, core)},
        {"sub": sub_at(3 - x, z, core)},
        {"grp": flip(g, 1)},
        {"grp": flip(g, 2)},
        {"grp": mirror(g)},
    ]
    bits = [core] + [lax.rem(z // b, 2) for b in (1, 2, 4)] + [lax.rem(x // b, 2) for b in (1, 2)]
    bits += [lax.rem(g // b, 2) for b in (1, 2, 4)]

    barrier = pltpu.get_barrier_semaphore()
    greet = partners + [{"sub": left}, {"sub": right}, {"sub": cross}]
    for who in greet:
        pl.semaphore_signal(barrier, inc=1, device_id=who, device_id_type=MESH)
    pl.semaphore_wait(barrier, len(greet))

    started = []

    def send(src, dst, ssem, rsem, who):
        copy = pltpu.make_async_remote_copy(
            src_ref=src, dst_ref=dst, send_sem=ssem, recv_sem=rsem, device_id=who, device_id_type=MESH
        )
        copy.start()
        started.append(copy)
        return copy

    def cols(which):
        return pl.ds(pl.multiple_of(which * 128, 128), 128)

    halos = []
    for i, k, who in ((0, 0, left), (1, 2, right)):
        halo_s[i] = mm_nt(wa[k], adj[...]).astype(BF)
        halos.append(send(halo_s.at[i], halo_r.at[i], halo_ss.at[i], halo_rs.at[i], {"sub": who}))
    firsts = [None] * 4

    def first(q):
        s0[q] = pan[q, :, cols(1 - core)].astype(BF)
        firsts[q] = send(s0.at[q], r0.at[q], ss0.at[q], rs0.at[q], {"sub": mate})

    pan[1] = mm(gl[1], om[...])
    first(1)
    pan[3] = mm_nt(gl[0], adj[...])
    first(3)
    pan[0] = mm(wf[:, 0:768], om_low[...]) + mm(wf[:, 768:1536], om[...]) + mm(wf[:, 1536:2304], om_high[...])
    first(0)
    own_adj = mm_nt(wa[1], adj[...])
    for copy in halos:
        copy.wait_recv()
    pan[2] = own_adj + halo_r[0].astype(F32) + halo_r[1].astype(F32)
    first(2)

    def split(value):
        top = value.astype(BF)
        return top, (value - top.astype(F32)).astype(BF)

    def twice(op, top, low):
        return mm(op, top) + mm(op, low)

    for ch in range(2):
        f_top, f_low = split(pan[2 * ch, :, cols(core)])
        o_top, o_low = split(pan[2 * ch + 1, :, cols(core)])
        own, far = ch * 2 + core, ch * 2 + 1 - core
        firsts[2 * ch + 1].wait_recv()
        o_far = r0[2 * ch + 1]
        o_new = twice(op_g[own][:, :K], o_top, o_low) + mm(op_g[far][:, :K], o_far)
        hi[0, 2 * ch + 1], lo[2 * ch + 1] = split(o_new)
        f_new = twice(op_s[own][:, :K], f_top, f_low) - twice(op_h[own][:, :K], o_top, o_low)
        f_new = f_new - mm(op_h[far][:, :K], o_far)
        firsts[2 * ch].wait_recv()
        f_new = f_new + mm(op_s[far][:, :K], r0[2 * ch])
        hi[0, 2 * ch], lo[2 * ch] = split(f_new)

    ways = []
    arrivals = []
    for i in (1, 0):
        ways.append(send(hi.at[0, 2 * (1 - z0) + i], rec.at[0, i], ss.at[0, i], rs.at[0, i], partners[1]))
    ways = [ways[1], ways[0]]
    for ch in range(2):
        out[0, ch, :, cols(core)] = hi[0, 2 * ch]
        arrivals.append(
            send(hi.at[0, 2 * ch], out.at[0, ch, :, cols(core)], os_s.at[0, ch], os_r.at[0, ch], partners[0])
        )
    f_top, o_top = hi[0, 2 * z0], hi[0, 2 * z0 + 1]
    f_low, o_low = lo[2 * z0], lo[2 * z0 + 1]
    peers = ({"sub": mate}, {"sub": zmate}, {"sub": cross})
    for j in range(1, LEVELS):
        base = (j * 2 + z0) * 2
        own, far = base + bits[j], base + 1 - bits[j]
        last = j == LEVELS - 1
        o_part = None if last else twice(op_g[own][:, :K], o_top, o_low)
        f_part = twice(op_s[own][:, :K], f_top, f_low) - twice(op_h[own][:, :K], o_top, o_low)
        ways[1].wait_recv()
        o_far = rec[j - 1, 1]
        nexts = [None, None]
        if not last:
            o_top, o_low = split(o_part + mm(op_g[far][:, :K], o_far))
            hi[j, 1] = o_top
            nexts[1] = send(hi.at[j, 1], rec.at[j, 1], ss.at[j, 1], rs.at[j, 1], partners[j + 1])
        f_part = f_part - mm(op_h[far][:, :K], o_far)
        ways[0].wait_recv()
        f_top, f_low = split(f_part + mm(op_s[far][:, :K], rec[j - 1, 0]))
        hi[j, 0] = f_top
        if not last:
            nexts[0] = send(hi.at[j, 0], rec.at[j, 0], ss.at[j, 0], rs.at[j, 0], partners[j + 1])
        for k, who in enumerate(peers):
            arrivals.append(
                send(hi.at[j, 0], out.at[j, z0, :, cols(core)], os_s.at[j, k], os_r.at[j, k], who)
            )
        out[j, z0, :, cols(core)] = f_top
        ways = nexts
    for copy in arrivals:
        copy.wait_recv()
    for copy in started:
        copy.wait_send()


def tree(*args):
    dma = pltpu.SemaphoreType.DMA
    return pl.pallas_call(
        tree_kernel,
        out_shape=jax.ShapeDtypeStruct((LEVELS, 2, K, 256), BF),
        in_specs=[vmem()] * len(args),
        out_specs=vmem(),
        scratch_shapes=[
            pltpu.VMEM((4, K, 256), F32),
            pltpu.VMEM((2, K, 256), BF),
            pltpu.VMEM((2, K, 256), BF),
            pltpu.VMEM((4, K, 128), BF),
            pltpu.VMEM((4, K, 128), BF),
            pltpu.VMEM((LEVELS, 4, K, 128), BF),
            pltpu.VMEM((4, K, 128), BF),
            pltpu.VMEM((LEVELS - 1, 2, K, 128), BF),
            dma((2,)),
            dma((2,)),
            dma((4,)),
            dma((4,)),
            dma((LEVELS, 2)),
            dma((LEVELS, 2)),
            dma((LEVELS, 3)),
            dma((LEVELS, 3)),
        ],
        compiler_params=pltpu.CompilerParams(
            collective_id=0, has_side_effects=True, vmem_limit_bytes=48 << 20
        ),
        name="tree",
    )(*args)


def local(omega, adj_tests, near_tiles, tile_cols, leaf_perms, leaf_interp, node_perms, node_maps):
    device = lax.axis_index("grp") * 64 + lax.axis_index("sub")
    up = [(i, (i + 1) % 64) for i in range(64)]
    down = [(b, a) for a, b in up]
    own_head = leaf_perms[0, 1, :K]
    cols_low = lax.ppermute(own_head, "sub", up)
    cols_high = lax.ppermute(own_head, "sub", down)
    om_low = lax.ppermute(omega, "sub", up)
    om_high = lax.ppermute(omega, "sub", down)
    adj = lax.all_to_all(adj_tests, "sub", split_axis=1, concat_axis=0, tiled=True)
    local_cols = tile_cols - (device - 1) * 6
    slots = jnp.arange(18, dtype=jnp.int32)
    counts = jnp.arange(1, 13, dtype=jnp.int32)
    inv = jnp.sum(
        jnp.where(local_cols[:, :, None] == slots[None, None, :], counts[None, :, None], 0), axis=1
    ).astype(jnp.int32)
    heads = jnp.stack([leaf_perms[0, 0, :K], own_head, cols_low, cols_high], axis=1)
    tails = leaf_perms[0, :, K:].T
    shifted = node_perms[0] + jnp.where(node_perms[0] >= K, 128 - K, 0)
    node_cols = shifted.transpose(0, 2, 1)
    ops = build(
        inv,
        heads,
        tails,
        node_cols,
        near_tiles.reshape(72, 128, 128),
        leaf_interp[0],
        node_maps.reshape(LEVELS * 4, K, K),
    )
    return tree(om_low, omega, om_high, adj, *ops)[None]


def solution(mesh):
    placed = (
        P(("grp", "sub"), None),
        P("sub", "grp"),
        P(("grp", "sub"), None, None, None),
        P(("grp", "sub"), None),
        P(("grp", "sub"), None, None),
        P(("grp", "sub"), None, None, None),
        P(("grp", "sub"), None, None, None),
        P(("grp", "sub"), None, None, None, None),
    )
    return jax.shard_map(
        local,
        mesh=mesh,
        in_specs=placed,
        out_specs=P(("grp", "sub"), None, None, None, None),
        check_vma=False,
    )
```

```python
import jax
import jax.numpy as jnp
from jax import lax
from jax.experimental import pallas as pl
from jax.experimental.pallas import tpu as pltpu
from jax.sharding import PartitionSpec as P

BF = jnp.bfloat16
F32 = jnp.float32
MESH = pl.DeviceIdType.MESH
K = 96
LEVELS = 9


def mm(a, b):
    return lax.dot_general(a, b, (((1,), (0,)), ((), ())), preferred_element_type=F32)


def mm_nt(a, b):
    return lax.dot_general(a, b, (((1,), (1,)), ((), ())), preferred_element_type=F32)


def mm_tn(a, b):
    return lax.dot_general(a, b, (((0,), (0,)), ((), ())), preferred_element_type=F32)


def onehot(column, width):
    lanes = lax.broadcasted_iota(jnp.int32, (column.shape[0], width), 1).astype(F32)
    return jnp.where(lanes == column, 1.0, 0.0)


def mirror(z):
    return lax.rem(jnp.where(lax.rem(z, 2) == 0, 14 - z, 16 - z), 8)


def flip(v, bit):
    return jnp.where(lax.rem(v // bit, 2) == 0, v + bit, v - bit)


def split(value):
    top = value.astype(BF)
    return top, (value - top.astype(F32)).astype(BF)


def twice(op, top, low):
    return mm(op, top) + mm(op, low)


def kernel(
    tile_cols, omega, tests, near_in, leaf_perms, interp_in, node_perms, maps_in,
    out,
    om, near, lperm, interp, nperm, maps, nrows, lrows, erows, orders, placed, wf, wa, gl, op_s, op_h, op_g,
    adj_in, adj, pan, halo_s, halo_r, s0, r0, hi, lo, rec,
    loc, a2a_s, a2a_r, near_ss, near_rs, halo_ss, halo_rs, ss0, rs0, ss, rs, os_s, os_r,
):
    g = lax.axis_index("grp")
    s = lax.axis_index("sub")
    core = lax.rem(s, 2)
    z = lax.rem(s // 2, 8)
    x = s // 16
    z0 = lax.rem(z, 2)
    left, right = lax.rem(s + 63, 64), lax.rem(s + 1, 64)

    def sub_at(xx, zz, cc):
        return (xx * 8 + zz) * 2 + cc

    mate = sub_at(x, z, 1 - core)
    zmate = sub_at(x, flip(z, 1), core)
    cross = sub_at(x, flip(z, 1), 1 - core)
    partners = [
        {"sub": mate},
        {"sub": zmate},
        {"sub": sub_at(x, flip(z, 2), core)},
        {"sub": sub_at(x, mirror(z), core)},
        {"sub": sub_at(flip(x, 1), z, core)},
        {"sub": sub_at(3 - x, z, core)},
        {"grp": flip(g, 1)},
        {"grp": flip(g, 2)},
        {"grp": mirror(g)},
    ]
    bits = [core] + [lax.rem(z // b, 2) for b in (1, 2, 4)] + [lax.rem(x // b, 2) for b in (1, 2)]
    bits += [lax.rem(g // b, 2) for b in (1, 2, 4)]

    def fetch(src, dst, i):
        copy = pltpu.make_async_copy(src, dst, loc.at[i])
        copy.start()
        return copy

    got_nperm = fetch(node_perms.at[0], nperm, 0)
    got_maps = fetch(maps_in.at[0], maps, 1)
    got_lperm = fetch(leaf_perms.at[0], lperm, 2)
    got_near = fetch(near_in, near, 3)
    got_interp = fetch(interp_in.at[0], interp, 4)
    got_om = fetch(omega, om.at[1], 5)
    own_tests = fetch(tests.at[:, pl.ds(pl.multiple_of(s * 768, 768), 768)], adj_in.at[s], 6)

    barrier = pltpu.get_barrier_semaphore()

    def greet(k, carry):
        pl.semaphore_signal(
            barrier, inc=1, device_id={"sub": lax.rem(s + k, 64)}, device_id_type=MESH
        )
        return carry

    lax.fori_loop(1, 64, greet, 0)
    for who in partners[6:]:
        pl.semaphore_signal(barrier, inc=1, device_id=who, device_id_type=MESH)

    got_nperm.wait()
    nrows[...] = jnp.zeros_like(nrows)
    for j in range(LEVELS):
        nrows[2 * j : 2 * j + 2, 0:192] = nperm[j].astype(F32)
    ncols = nrows[...].T
    ncols = ncols + jnp.where(ncols >= K, 128.0 - K, 0.0)
    got_maps.wait()
    for j in range(LEVELS):
        picks = [onehot(ncols[0:192, 2 * j + i : 2 * j + i + 1], 256) for i in range(2)]
        low_high, high_low = maps[j, 2], maps[j, 3]
        for ch in range(2):
            sel = picks[ch][:K].astype(BF)
            rows = picks[1 - ch]
            full = (rows[:K] + mm_tn(maps[j, 1 - ch], rows[K:].astype(BF))).astype(BF)
            couple = (high_low, low_high) if ch == 0 else (low_high, high_low)
            times = mm if ch == 0 else mm_nt
            for half in range(2):
                at = (j * 2 + ch) * 2 + half
                op_s[at] = sel[:, half * 128 : half * 128 + 128]
                op_g[at] = full[:, half * 128 : half * 128 + 128]
                other = sel[:, (1 - half) * 128 : (1 - half) * 128 + K]
                op_h[at, :, 0:K] = times(other, couple[half]).astype(BF)

    pl.semaphore_wait(barrier, 66)

    started = []

    def send(src, dst, ssem, rsem, who):
        copy = pltpu.make_async_remote_copy(
            src_ref=src, dst_ref=dst, send_sem=ssem, recv_sem=rsem, device_id=who, device_id_type=MESH
        )
        copy.start()
        started.append(copy)
        return copy

    def trade(k):
        peer = lax.rem(s + k, 64)
        return pltpu.make_async_remote_copy(
            src_ref=tests.at[:, pl.ds(pl.multiple_of(peer * 768, 768), 768)],
            dst_ref=adj_in.at[s],
            send_sem=a2a_s.at[peer],
            recv_sem=a2a_r.at[s],
            device_id={"sub": peer},
            device_id_type=MESH,
        )

    got_orders, got_omega = [None, None], [None, None]
    for i, who in ((0, right), (1, left)):
        got_orders[i] = send(leaf_perms.at[0], orders.at[i], near_ss.at[i], near_rs.at[i], {"sub": who})

    def trade_start(k, carry):
        trade(k).start()
        return carry

    lax.fori_loop(1, 64, trade_start, 0)
    for i, who in ((0, right), (1, left)):
        got_omega[i] = send(omega, om.at[2 * i], near_ss.at[2 + i], near_rs.at[2 + i], {"sub": who})

    def cols(which):
        return pl.ds(pl.multiple_of(which * 128, 128), 128)

    got_near.wait()
    base = ((g * 64 + s) - 1) * 6

    def place(q, carry):
        held = [tile_cols[q, t] - base for t in range(12)]
        for m in range(18):
            at = 0
            for t in range(12):
                at = jnp.where(held[t] == m, t + 1, at)
            tile = near[q, jnp.maximum(at - 1, 0)]
            keep = jnp.where(at > 0, 1.0, 0.0)
            placed[pl.ds(pl.multiple_of(q * 128, 128), 128), m * 128 : (m + 1) * 128] = tile * keep.astype(BF)
        return carry

    lax.fori_loop(0, 6, place, 0)
    got_lperm.wait()
    lrows[...] = jnp.zeros_like(lrows)
    lrows[0:2] = lperm[...].astype(F32)
    lcols = lrows[...].T
    wf[...] = mm(onehot(lcols[0:K, 0:1], 768).astype(BF), placed[...]).astype(BF)
    got_interp.wait()
    for i in range(2):
        tail = onehot(lcols[K:768, i : i + 1], 768).astype(BF)
        gl[i] = (onehot(lcols[0:K, i : i + 1], 768) + mm(interp[i], tail)).astype(BF)
    erows[...] = jnp.zeros_like(erows)
    for i in range(2):
        got_orders[i].wait_recv()
        erows[i : i + 1] = orders[i, 1:2, 0:128].astype(F32)
    ecols = erows[...].T
    for k, col in enumerate((ecols[0:K, 0:1], lcols[0:K, 1:2], ecols[0:K, 1:2])):
        wa[k] = mm_nt(onehot(col, 768).astype(BF), placed[:, k * 768 : (k + 1) * 768]).astype(BF)

    firsts = [None] * 4

    def first(q):
        s0[q] = pan[q, :, cols(1 - core)].astype(BF)
        firsts[q] = send(s0.at[q], r0.at[q], ss0.at[q], rs0.at[q], {"sub": mate})

    got_om.wait()
    pan[1] = mm(gl[1], om[1])
    first(1)
    total = mm(wf[:, 768:1536], om[1])
    for i in range(2):
        got_omega[i].wait_recv()
        total = total + mm(wf[:, i * 1536 : i * 1536 + 768], om[2 * i])
    pan[0] = total
    first(0)

    own_tests.wait()

    def trade_wait(k, carry):
        peer = lax.rem(s + k, 64)
        pltpu.make_async_remote_copy(
            src_ref=adj_in.at[peer],
            dst_ref=adj_in.at[peer],
            send_sem=a2a_s.at[peer],
            recv_sem=a2a_r.at[peer],
            device_id={"sub": peer},
            device_id_type=MESH,
        ).wait_recv()
        return carry

    lax.fori_loop(1, 64, trade_wait, 0)
    adj[...] = adj_in[...].reshape(256, 768)
    halos = []
    for i, k, who in ((0, 0, left), (1, 2, right)):
        halo_s[i] = mm_nt(wa[k], adj[...]).astype(BF)
        halos.append(send(halo_s.at[i], halo_r.at[i], halo_ss.at[i], halo_rs.at[i], {"sub": who}))
    pan[3] = mm_nt(gl[0], adj[...])
    first(3)
    own_adj = mm_nt(wa[1], adj[...])
    for copy in halos:
        copy.wait_recv()
    pan[2] = own_adj + halo_r[0].astype(F32) + halo_r[1].astype(F32)
    first(2)

    for ch in range(2):
        f_top, f_low = split(pan[2 * ch, :, cols(core)])
        o_top, o_low = split(pan[2 * ch + 1, :, cols(core)])
        own, far = ch * 2 + core, ch * 2 + 1 - core
        firsts[2 * ch + 1].wait_recv()
        o_far = r0[2 * ch + 1]
        o_new = twice(op_g[own][:, :K], o_top, o_low) + mm(op_g[far][:, :K], o_far)
        hi[0, 2 * ch + 1], lo[2 * ch + 1] = split(o_new)
        f_new = twice(op_s[own][:, :K], f_top, f_low) - twice(op_h[own][:, :K], o_top, o_low)
        f_new = f_new - mm(op_h[far][:, :K], o_far)
        firsts[2 * ch].wait_recv()
        f_new = f_new + mm(op_s[far][:, :K], r0[2 * ch])
        hi[0, 2 * ch], lo[2 * ch] = split(f_new)

    ways = []
    arrivals = []
    for i in (1, 0):
        ways.append(send(hi.at[0, 2 * (1 - z0) + i], rec.at[0, i], ss.at[0, i], rs.at[0, i], partners[1]))
    ways = [ways[1], ways[0]]
    for ch in range(2):
        out[0, ch, :, cols(core)] = hi[0, 2 * ch]
        arrivals.append(
            send(hi.at[0, 2 * ch], out.at[0, ch, :, cols(core)], os_s.at[0, ch], os_r.at[0, ch], partners[0])
        )
    f_top, o_top = hi[0, 2 * z0], hi[0, 2 * z0 + 1]
    f_low, o_low = lo[2 * z0], lo[2 * z0 + 1]
    peers = ({"sub": mate}, {"sub": zmate}, {"sub": cross})
    for j in range(1, LEVELS):
        base = (j * 2 + z0) * 2
        own, far = base + bits[j], base + 1 - bits[j]
        last = j == LEVELS - 1
        o_part = None if last else twice(op_g[own][:, :K], o_top, o_low)
        f_part = twice(op_s[own][:, :K], f_top, f_low) - twice(op_h[own][:, :K], o_top, o_low)
        ways[1].wait_recv()
        o_far = rec[j - 1, 1]
        nexts = [None, None]
        if not last:
            o_top, o_low = split(o_part + mm(op_g[far][:, :K], o_far))
            hi[j, 1] = o_top
            nexts[1] = send(hi.at[j, 1], rec.at[j, 1], ss.at[j, 1], rs.at[j, 1], partners[j + 1])
        f_part = f_part - mm(op_h[far][:, :K], o_far)
        ways[0].wait_recv()
        f_top, f_low = split(f_part + mm(op_s[far][:, :K], rec[j - 1, 0]))
        hi[j, 0] = f_top
        if not last:
            nexts[0] = send(hi.at[j, 0], rec.at[j, 0], ss.at[j, 0], rs.at[j, 0], partners[j + 1])
        for k, who in enumerate(peers):
            arrivals.append(
                send(hi.at[j, 0], out.at[j, z0, :, cols(core)], os_s.at[j, k], os_r.at[j, k], who)
            )
        out[j, z0, :, cols(core)] = f_top
        ways = nexts
    for copy in arrivals:
        copy.wait_recv()
    for copy in started:
        copy.wait_send()

    def trade_end(k, carry):
        trade(k).wait_send()
        return carry

    lax.fori_loop(1, 64, trade_end, 0)


def local(omega, adj_tests, near_tiles, tile_cols, leaf_perms, leaf_interp, node_perms, node_maps):
    dma = pltpu.SemaphoreType.DMA
    anywhere = pl.BlockSpec(memory_space=pl.ANY)
    ops = pltpu.VMEM((LEVELS * 4, K, 128), BF)
    return pl.pallas_call(
        kernel,
        out_shape=jax.ShapeDtypeStruct((LEVELS, 2, K, 256), BF),
        in_specs=[pl.BlockSpec(memory_space=pltpu.SMEM)] + [anywhere] * 7,
        out_specs=pl.BlockSpec(memory_space=pltpu.VMEM),
        scratch_shapes=[
            pltpu.VMEM((3, 768, 256), BF),
            pltpu.VMEM((6, 12, 128, 128), BF),
            pltpu.VMEM((2, 768), jnp.int32),
            pltpu.VMEM((2, K, 672), BF),
            pltpu.VMEM((LEVELS, 2, 192), jnp.int32),
            pltpu.VMEM((LEVELS, 4, K, K), BF),
            pltpu.VMEM((24, 256), F32),
            pltpu.VMEM((8, 768), F32),
            pltpu.VMEM((8, 128), F32),
            pltpu.VMEM((2, 2, 768), jnp.int32),
            pltpu.VMEM((768, 2304), BF),
            pltpu.VMEM((K, 2304), BF),
            pltpu.VMEM((3, K, 768), BF),
            pltpu.VMEM((2, K, 768), BF),
            ops,
            ops,
            ops,
            pltpu.VMEM((64, 4, 768), BF),
            pltpu.VMEM((256, 768), BF),
            pltpu.VMEM((4, K, 256), F32),
            pltpu.VMEM((2, K, 256), BF),
            pltpu.VMEM((2, K, 256), BF),
            pltpu.VMEM((4, K, 128), BF),
            pltpu.VMEM((4, K, 128), BF),
            pltpu.VMEM((LEVELS, 4, K, 128), BF),
            pltpu.VMEM((4, K, 128), BF),
            pltpu.VMEM((LEVELS - 1, 2, K, 128), BF),
            dma((7,)),
            dma((64,)),
            dma((64,)),
            dma((4,)),
            dma((4,)),
            dma((2,)),
            dma((2,)),
            dma((4,)),
            dma((4,)),
            dma((LEVELS, 2)),
            dma((LEVELS, 2)),
            dma((LEVELS, 3)),
            dma((LEVELS, 3)),
        ],
        compiler_params=pltpu.CompilerParams(
            collective_id=0, has_side_effects=True, vmem_limit_bytes=56 << 20
        ),
        name="window",
    )(
        tile_cols,
        omega,
        adj_tests,
        near_tiles,
        leaf_perms,
        jnp.swapaxes(leaf_interp, 2, 3),
        node_perms,
        node_maps,
    )[None]


def solution(mesh):
    placed = (
        P(("grp", "sub"), None),
        P("sub", "grp"),
        P(("grp", "sub"), None, None, None),
        P(("grp", "sub"), None),
        P(("grp", "sub"), None, None),
        P(("grp", "sub"), None, None, None),
        P(("grp", "sub"), None, None, None),
        P(("grp", "sub"), None, None, None, None),
    )
    return jax.shard_map(
        local,
        mesh=mesh,
        in_specs=placed,
        out_specs=P(("grp", "sub"), None, None, None, None),
        check_vma=False,
    )
```

```python
import jax
import jax.numpy as jnp
from jax import lax
from jax.experimental import pallas as pl
from jax.experimental.pallas import tpu as pltpu
from jax.sharding import PartitionSpec as P

BF = jnp.bfloat16
F32 = jnp.float32
MESH = pl.DeviceIdType.MESH
K = 96
LEVELS = 9


def mm(a, b):
    return lax.dot_general(a, b, (((1,), (0,)), ((), ())), preferred_element_type=F32)


def mm_nt(a, b):
    return lax.dot_general(a, b, (((1,), (1,)), ((), ())), preferred_element_type=F32)


def mm_tn(a, b):
    return lax.dot_general(a, b, (((0,), (0,)), ((), ())), preferred_element_type=F32)


def onehot(column, width):
    lanes = lax.broadcasted_iota(jnp.int32, (column.shape[0], width), 1).astype(F32)
    return jnp.where(lanes == column, 1.0, 0.0)


def mirror(z):
    return lax.rem(jnp.where(lax.rem(z, 2) == 0, 14 - z, 16 - z), 8)


def flip(v, bit):
    return jnp.where(lax.rem(v // bit, 2) == 0, v + bit, v - bit)


def split(value):
    top = value.astype(BF)
    return top, (value - top.astype(F32)).astype(BF)


def twice(op, top, low):
    return mm(op, top) + mm(op, low)


def kernel(
    tile_cols, omega, tests, near_in, leaf_perms, interp_in, node_perms, maps_in,
    out,
    om, om_mate, w_in, near, lperm, interp, nperm, maps, nrows, lrows, erows, orders, placed, wf, wa, gl, op_s, op_h, op_g,
    adj_in, adj, pan, pan_far, d_s, d_r, s0, r0, hi, lo, rec,
    loc, a2a_s, a2a_r, near_ss, near_rs, d_ss, d_rs, ss0, rs0, ss, rs, os_s, os_r,
):
    g = lax.axis_index("grp")
    s = lax.axis_index("sub")
    core = lax.rem(s, 2)
    z = lax.rem(s // 2, 8)
    x = s // 16
    z0 = lax.rem(z, 2)
    left, right = lax.rem(s + 63, 64), lax.rem(s + 1, 64)
    outer = lax.rem(s + 63 + 2 * core, 64)
    outer_twin = lax.rem(s + 62 + 4 * core, 64)

    def sub_at(xx, zz, cc):
        return (xx * 8 + zz) * 2 + cc

    mate = sub_at(x, z, 1 - core)
    zmate = sub_at(x, flip(z, 1), core)
    cross = sub_at(x, flip(z, 1), 1 - core)
    partners = [
        {"sub": mate},
        {"sub": zmate},
        {"sub": sub_at(x, flip(z, 2), core)},
        {"sub": sub_at(x, mirror(z), core)},
        {"sub": sub_at(flip(x, 1), z, core)},
        {"sub": sub_at(3 - x, z, core)},
        {"grp": flip(g, 1)},
        {"grp": flip(g, 2)},
        {"grp": mirror(g)},
    ]
    bits = [core] + [lax.rem(z // b, 2) for b in (1, 2, 4)] + [lax.rem(x // b, 2) for b in (1, 2)]
    bits += [lax.rem(g // b, 2) for b in (1, 2, 4)]

    def fetch(src, dst, i):
        copy = pltpu.make_async_copy(src, dst, loc.at[i])
        copy.start()
        return copy

    got_nperm = fetch(node_perms.at[0], nperm, 0)
    got_maps = fetch(maps_in.at[0], maps, 1)
    got_lperm = fetch(leaf_perms.at[0], lperm, 2)
    got_near = fetch(near_in, near, 3)
    got_interp = fetch(interp_in.at[0], interp, 4)
    got_om = fetch(omega, om, 5)
    own_tests = fetch(tests.at[:, pl.ds(pl.multiple_of(s * 768, 768), 768)], adj_in.at[s], 6)

    barrier = pltpu.get_barrier_semaphore()

    def greet(k, carry):
        pl.semaphore_signal(
            barrier, inc=1, device_id={"sub": lax.rem(s + k, 64)}, device_id_type=MESH
        )
        return carry

    lax.fori_loop(1, 64, greet, 0)
    for who in partners[6:]:
        pl.semaphore_signal(barrier, inc=1, device_id=who, device_id_type=MESH)

    got_nperm.wait()
    nrows[...] = jnp.zeros_like(nrows)
    for j in range(LEVELS):
        nrows[2 * j : 2 * j + 2, 0:192] = nperm[j].astype(F32)
    ncols = nrows[...].T
    ncols = ncols + jnp.where(ncols >= K, 128.0 - K, 0.0)
    got_maps.wait()
    for j in range(LEVELS):
        picks = [onehot(ncols[0:192, 2 * j + i : 2 * j + i + 1], 256) for i in range(2)]
        low_high, high_low = maps[j, 2], maps[j, 3]
        for ch in range(2):
            sel = picks[ch][:K].astype(BF)
            rows = picks[1 - ch]
            full = (rows[:K] + mm_tn(maps[j, 1 - ch], rows[K:].astype(BF))).astype(BF)
            couple = (high_low, low_high) if ch == 0 else (low_high, high_low)
            times = mm if ch == 0 else mm_nt
            for half in range(2):
                at = (j * 2 + ch) * 2 + half
                op_s[at] = sel[:, half * 128 : half * 128 + 128]
                op_g[at] = full[:, half * 128 : half * 128 + 128]
                other = sel[:, (1 - half) * 128 : (1 - half) * 128 + K]
                op_h[at, :, 0:K] = times(other, couple[half]).astype(BF)

    pl.semaphore_wait(barrier, 66)

    started = []

    def send(src, dst, ssem, rsem, who):
        copy = pltpu.make_async_remote_copy(
            src_ref=src, dst_ref=dst, send_sem=ssem, recv_sem=rsem, device_id=who, device_id_type=MESH
        )
        copy.start()
        started.append(copy)
        return copy

    def trade(k):
        peer = lax.rem(s + k, 64)
        return pltpu.make_async_remote_copy(
            src_ref=tests.at[:, pl.ds(pl.multiple_of(peer * 768, 768), 768)],
            dst_ref=adj_in.at[s],
            send_sem=a2a_s,
            recv_sem=a2a_r,
            device_id={"sub": peer},
            device_id_type=MESH,
        )

    got_orders = [None, None]
    for i, who in ((0, right), (1, left)):
        got_orders[i] = send(leaf_perms.at[0], orders.at[i], near_ss.at[i], near_rs.at[i], {"sub": who})
    got_mate = send(omega, om_mate, near_ss.at[2], near_rs.at[2], {"sub": mate})

    def trade_start(k, carry):
        trade(k).start()
        return carry

    lax.fori_loop(1, 64, trade_start, 0)

    def cols(which):
        return pl.ds(pl.multiple_of(which * 128, 128), 128)

    got_lperm.wait()
    lrows[...] = jnp.zeros_like(lrows)
    lrows[0:2] = lperm[...].astype(F32)
    lcols = lrows[...].T
    base = ((g * 64 + s) - 1) * 6
    got_near.wait()

    def place(q, carry):
        held = [tile_cols[q, t] - base for t in range(12)]
        for m in range(18):
            at = 0
            for t in range(12):
                at = jnp.where(held[t] == m, t + 1, at)
            tile = near[q, jnp.maximum(at - 1, 0)]
            keep = jnp.where(at > 0, 1.0, 0.0)
            placed[pl.ds(pl.multiple_of(q * 128, 128), 128), m * 128 : (m + 1) * 128] = tile * keep.astype(BF)
        return carry

    lax.fori_loop(0, 6, place, 0)
    picked = onehot(lcols[0:K, 0:1], 768).astype(BF)
    for k in range(3):
        wf[k] = mm(picked, placed[:, k * 768 : (k + 1) * 768]).astype(BF)
    got_w = send(wf.at[2 * core], w_in, near_ss.at[3], near_rs.at[3], {"sub": outer})

    firsts = [None] * 5

    def first(q, value):
        s0[q] = value.astype(BF)
        firsts[q] = send(s0.at[q], r0.at[q], ss0.at[q], rs0.at[q], {"sub": mate})

    def outward(i, value):
        for half in range(2):
            d_s[i, half] = value[:, half * 128 : half * 128 + 128].astype(BF)
        copies = []
        for n, (half, who) in enumerate(((1 - core, outer), (core, outer_twin))):
            copies.append(
                send(d_s.at[i, half], d_r.at[i, 1 - core], d_ss.at[i, n], d_rs.at[i, 1 - core], {"sub": who})
            )
        return copies

    def outward_done(i):
        for slot in range(2):
            pltpu.make_async_remote_copy(
                src_ref=d_s.at[i, slot],
                dst_ref=d_r.at[i, slot],
                send_sem=d_ss.at[i, slot],
                recv_sem=d_rs.at[i, slot],
                device_id={"sub": outer},
                device_id_type=MESH,
            ).wait_recv()

    got_interp.wait()
    for i in (1, 0):
        tail = onehot(lcols[K:768, i : i + 1], 768).astype(BF)
        gl[i] = (onehot(lcols[0:K, i : i + 1], 768) + mm(interp[i], tail)).astype(BF)
    got_om.wait()
    pan[1] = mm(gl[1], om[...])
    first(1, pan[1, :, cols(1 - core)])
    got_mate.wait_recv()
    pan[0] = mm(wf[1], om[...]) + mm(wf[2 * (1 - core)], om_mate[...])
    first(0, pan[0, :, cols(1 - core)])
    erows[...] = jnp.zeros_like(erows)
    for i in range(2):
        got_orders[i].wait_recv()
        erows[i : i + 1] = orders[i, 1:2, 0:128].astype(F32)
    ecols = erows[...].T
    for k, col in enumerate((ecols[0:K, 0:1], lcols[0:K, 1:2], ecols[0:K, 1:2])):
        wa[k] = mm_nt(onehot(col, 768).astype(BF), placed[:, k * 768 : (k + 1) * 768]).astype(BF)
    got_w.wait_recv()
    outward(0, mm(w_in[...], om[...]))

    def chain_send(ch, i):
        return pltpu.make_async_remote_copy(
            src_ref=hi.at[0, 2 * ch + i],
            dst_ref=rec.at[0, i],
            send_sem=ss.at[0, i],
            recv_sem=rs.at[0, i],
            device_id=partners[1],
            device_id_type=MESH,
        )

    def chain_start(ch, i):
        @pl.when(z0 == 1 - ch)
        def _():
            chain_send(ch, i).start()

    def tests_up(ch):
        own, far = ch * 2 + core, ch * 2 + 1 - core
        q = 2 * ch + 1
        top, low = split(pan[q, :, cols(core)])
        firsts[q].wait_recv()
        top_new, lo[q] = split(twice(op_g[own][:, :K], top, low) + mm(op_g[far][:, :K], r0[q]))
        hi[0, q] = top_new
        chain_start(ch, 1)
        return twice(op_h[own][:, :K], top, low) + mm(op_h[far][:, :K], r0[q])

    def rows_up(ch, coupled, own_rows, far_rows):
        own, far = ch * 2 + core, ch * 2 + 1 - core
        new = twice(op_s[own][:, :K], *split(own_rows)) + twice(op_s[far][:, :K], *split(far_rows)) - coupled
        top_new, lo[2 * ch] = split(new)
        hi[0, 2 * ch] = top_new
        chain_start(ch, 0)
        out[0, ch, :, cols(core)] = top_new
        arrivals.append(
            send(hi.at[0, 2 * ch], out.at[0, ch, :, cols(core)], os_s.at[0, ch], os_r.at[0, ch], partners[0])
        )

    arrivals = []
    coupled_fwd = tests_up(0)

    own_tests.wait()
    everyone = adj_in.at[pl.ds(0, 63)]
    trades = pltpu.make_async_remote_copy(
        src_ref=everyone,
        dst_ref=everyone,
        send_sem=a2a_s,
        recv_sem=a2a_r,
        device_id={"sub": right},
        device_id_type=MESH,
    )
    trades.wait_recv()
    adj[...] = adj_in[...].reshape(256, 768)
    outward(1, mm_nt(wa[2 * core], adj[...]))
    pan[3] = mm_nt(gl[0], adj[...])
    first(3, pan[3, :, cols(1 - core)])
    pan[2] = mm_nt(wa[1], adj[...])
    first(4, pan[2, :, cols(1 - core)])
    pan_far[...] = mm_nt(wa[2 * (1 - core)], adj[...])
    first(2, pan_far[:, cols(1 - core)])
    firsts[0].wait_recv()
    outward_done(0)
    rows_up(
        0,
        coupled_fwd,
        pan[0, :, cols(core)] + d_r[0, core].astype(F32),
        r0[0].astype(F32) + d_r[0, 1 - core].astype(F32),
    )
    coupled_adj = tests_up(1)
    firsts[2].wait_recv()
    firsts[4].wait_recv()
    outward_done(1)
    rows_up(
        1,
        coupled_adj,
        pan[2, :, cols(core)] + r0[2].astype(F32) + d_r[1, core].astype(F32),
        pan_far[:, cols(core)] + r0[4].astype(F32) + d_r[1, 1 - core].astype(F32),
    )
    ways = [chain_send(0, 0), chain_send(0, 1)]
    started += ways
    f_top, o_top = hi[0, 2 * z0], hi[0, 2 * z0 + 1]
    f_low, o_low = lo[2 * z0], lo[2 * z0 + 1]
    peers = ({"sub": mate}, {"sub": zmate}, {"sub": cross})
    for j in range(1, LEVELS):
        base = (j * 2 + z0) * 2
        own, far = base + bits[j], base + 1 - bits[j]
        last = j == LEVELS - 1
        o_part = None if last else twice(op_g[own][:, :K], o_top, o_low)
        f_part = twice(op_s[own][:, :K], f_top, f_low) - twice(op_h[own][:, :K], o_top, o_low)
        ways[1].wait_recv()
        o_far = rec[j - 1, 1]
        nexts = [None, None]
        if not last:
            o_top, o_low = split(o_part + mm(op_g[far][:, :K], o_far))
            hi[j, 1] = o_top
            nexts[1] = send(hi.at[j, 1], rec.at[j, 1], ss.at[j, 1], rs.at[j, 1], partners[j + 1])
        f_part = f_part - mm(op_h[far][:, :K], o_far)
        ways[0].wait_recv()
        f_top, f_low = split(f_part + mm(op_s[far][:, :K], rec[j - 1, 0]))
        hi[j, 0] = f_top
        if not last:
            nexts[0] = send(hi.at[j, 0], rec.at[j, 0], ss.at[j, 0], rs.at[j, 0], partners[j + 1])
        for k, who in enumerate(peers):
            arrivals.append(
                send(hi.at[j, 0], out.at[j, z0, :, cols(core)], os_s.at[j, k], os_r.at[j, k], who)
            )
        out[j, z0, :, cols(core)] = f_top
        ways = nexts
    for copy in arrivals:
        copy.wait_recv()
    for copy in started:
        copy.wait_send()

    trades.wait_send()


def local(omega, adj_tests, near_tiles, tile_cols, leaf_perms, leaf_interp, node_perms, node_maps):
    dma = pltpu.SemaphoreType.DMA
    anywhere = pl.BlockSpec(memory_space=pl.ANY)
    ops = pltpu.VMEM((LEVELS * 4, K, 128), BF)
    return pl.pallas_call(
        kernel,
        out_shape=jax.ShapeDtypeStruct((LEVELS, 2, K, 256), BF),
        in_specs=[pl.BlockSpec(memory_space=pltpu.SMEM)] + [anywhere] * 7,
        out_specs=pl.BlockSpec(memory_space=pltpu.VMEM),
        scratch_shapes=[
            pltpu.VMEM((768, 256), BF),
            pltpu.VMEM((768, 256), BF),
            pltpu.VMEM((K, 768), BF),
            pltpu.VMEM((6, 12, 128, 128), BF),
            pltpu.VMEM((2, 768), jnp.int32),
            pltpu.VMEM((2, K, 672), BF),
            pltpu.VMEM((LEVELS, 2, 192), jnp.int32),
            pltpu.VMEM((LEVELS, 4, K, K), BF),
            pltpu.VMEM((24, 256), F32),
            pltpu.VMEM((8, 768), F32),
            pltpu.VMEM((8, 128), F32),
            pltpu.VMEM((2, 2, 768), jnp.int32),
            pltpu.VMEM((768, 2304), BF),
            pltpu.VMEM((3, K, 768), BF),
            pltpu.VMEM((3, K, 768), BF),
            pltpu.VMEM((2, K, 768), BF),
            ops,
            ops,
            ops,
            pltpu.VMEM((64, 4, 768), BF),
            pltpu.VMEM((256, 768), BF),
            pltpu.VMEM((4, K, 256), F32),
            pltpu.VMEM((K, 256), F32),
            pltpu.VMEM((2, 2, K, 128), BF),
            pltpu.VMEM((2, 2, K, 128), BF),
            pltpu.VMEM((5, K, 128), BF),
            pltpu.VMEM((5, K, 128), BF),
            pltpu.VMEM((LEVELS, 4, K, 128), BF),
            pltpu.VMEM((4, K, 128), BF),
            pltpu.VMEM((LEVELS - 1, 2, K, 128), BF),
            dma((7,)),
            dma,
            dma,
            dma((4,)),
            dma((4,)),
            dma((2, 2)),
            dma((2, 2)),
            dma((5,)),
            dma((5,)),
            dma((LEVELS, 2)),
            dma((LEVELS, 2)),
            dma((LEVELS, 3)),
            dma((LEVELS, 3)),
        ],
        compiler_params=pltpu.CompilerParams(
            collective_id=0, has_side_effects=True, vmem_limit_bytes=56 << 20
        ),
        name="window",
    )(
        tile_cols,
        omega,
        adj_tests,
        near_tiles,
        leaf_perms,
        jnp.swapaxes(leaf_interp, 2, 3),
        node_perms,
        node_maps,
    )[None]


def solution(mesh):
    placed = (
        P(("grp", "sub"), None),
        P("sub", "grp"),
        P(("grp", "sub"), None, None, None),
        P(("grp", "sub"), None),
        P(("grp", "sub"), None, None),
        P(("grp", "sub"), None, None, None),
        P(("grp", "sub"), None, None, None),
        P(("grp", "sub"), None, None, None, None),
    )
    return jax.shard_map(
        local,
        mesh=mesh,
        in_specs=placed,
        out_specs=P(("grp", "sub"), None, None, None, None),
        check_vma=False,
    )
```

```python
import jax
import jax.numpy as jnp
from jax import lax
from jax.experimental import pallas as pl
from jax.experimental.pallas import tpu as pltpu
from jax.sharding import PartitionSpec as P

BF = jnp.bfloat16
F32 = jnp.float32
MESH = pl.DeviceIdType.MESH
K = 96
LEVELS = 9


def mm(a, b):
    return lax.dot_general(a, b, (((1,), (0,)), ((), ())), preferred_element_type=F32)


def mm_nt(a, b):
    return lax.dot_general(a, b, (((1,), (1,)), ((), ())), preferred_element_type=F32)


def mm_tn(a, b):
    return lax.dot_general(a, b, (((0,), (0,)), ((), ())), preferred_element_type=F32)


def onehot(column, width):
    lanes = lax.broadcasted_iota(jnp.int32, (column.shape[0], width), 1).astype(F32)
    return jnp.where(lanes == column, 1.0, 0.0)


def mirror(z):
    return lax.rem(jnp.where(lax.rem(z, 2) == 0, 14 - z, 16 - z), 8)


def flip(v, bit):
    return jnp.where(lax.rem(v // bit, 2) == 0, v + bit, v - bit)


def split(value):
    top = value.astype(BF)
    return top, (value - top.astype(F32)).astype(BF)


def twice(op, top, low):
    return mm(op, top) + mm(op, low)


def kernel(
    tile_cols, omega, tests, near_in, leaf_perms, interp_in, node_perms, maps_in,
    out,
    om, om_mate, w_in, near, lperm, interp, nperm, maps, nrows, lrows, erows, orders, placed, wf, wa, gl, op_s, op_h, op_g,
    adj_in, adj, pan, pan_far, d_s, d_r, s0, r0, hi, lo, rec, fin_s, fin_r,
    loc, a2a_s, a2a_r, near_ss, near_rs, d_ss, d_rs, ss0, rs0, ss, rs, os_s, os_r, fin_ss, fin_rs,
):
    g = lax.axis_index("grp")
    s = lax.axis_index("sub")
    core = lax.rem(s, 2)
    z = lax.rem(s // 2, 8)
    x = s // 16
    z0 = lax.rem(z, 2)
    left, right = lax.rem(s + 63, 64), lax.rem(s + 1, 64)
    outer = lax.rem(s + 63 + 2 * core, 64)
    outer_twin = lax.rem(s + 62 + 4 * core, 64)

    def sub_at(xx, zz, cc):
        return (xx * 8 + zz) * 2 + cc

    mate = sub_at(x, z, 1 - core)
    zmate = sub_at(x, flip(z, 1), core)
    cross = sub_at(x, flip(z, 1), 1 - core)
    partners = [
        {"sub": mate},
        {"sub": zmate},
        {"sub": sub_at(x, flip(z, 2), core)},
        {"sub": sub_at(x, mirror(z), core)},
        {"sub": sub_at(flip(x, 1), z, core)},
        {"sub": sub_at(3 - x, z, core)},
        {"grp": flip(g, 1)},
        {"grp": flip(g, 2)},
        {"grp": mirror(g)},
        {"grp": jnp.where(lax.rem(g // 2, 2) == 0, 5 - g, 9 - g)},
    ]
    bits = [core] + [lax.rem(z // b, 2) for b in (1, 2, 4)] + [lax.rem(x // b, 2) for b in (1, 2)]
    bits += [lax.rem(g // b, 2) for b in (1, 2, 4)]

    def fetch(src, dst, i):
        copy = pltpu.make_async_copy(src, dst, loc.at[i])
        copy.start()
        return copy

    got_nperm = fetch(node_perms.at[0], nperm, 0)
    got_maps = fetch(maps_in.at[0], maps, 1)
    got_lperm = fetch(leaf_perms.at[0], lperm, 2)
    got_near = fetch(near_in, near, 3)
    got_interp = fetch(interp_in.at[0], interp, 4)
    got_om = fetch(omega, om, 5)
    own_tests = fetch(tests.at[:, pl.ds(pl.multiple_of(s * 768, 768), 768)], adj_in.at[s], 6)

    barrier = pltpu.get_barrier_semaphore()

    def greet(k, carry):
        pl.semaphore_signal(
            barrier, inc=1, device_id={"sub": lax.rem(s + k, 64)}, device_id_type=MESH
        )
        return carry

    lax.fori_loop(1, 64, greet, 0)
    for who in partners[6:]:
        pl.semaphore_signal(barrier, inc=1, device_id=who, device_id_type=MESH)

    got_nperm.wait()
    nrows[...] = jnp.zeros_like(nrows)
    for j in range(LEVELS):
        nrows[2 * j : 2 * j + 2, 0:192] = nperm[j].astype(F32)
    ncols = nrows[...].T
    ncols = ncols + jnp.where(ncols >= K, 128.0 - K, 0.0)
    got_maps.wait()
    for j in range(LEVELS):
        picks = [onehot(ncols[0:192, 2 * j + i : 2 * j + i + 1], 256) for i in range(2)]
        low_high, high_low = maps[j, 2], maps[j, 3]
        for ch in range(2):
            sel = picks[ch][:K].astype(BF)
            rows = picks[1 - ch]
            full = (rows[:K] + mm_tn(maps[j, 1 - ch], rows[K:].astype(BF))).astype(BF)
            couple = (high_low, low_high) if ch == 0 else (low_high, high_low)
            times = mm if ch == 0 else mm_nt
            for half in range(2):
                at = (j * 2 + ch) * 2 + half
                op_s[at] = sel[:, half * 128 : half * 128 + 128]
                op_g[at] = full[:, half * 128 : half * 128 + 128]
                other = sel[:, (1 - half) * 128 : (1 - half) * 128 + K]
                op_h[at, :, 0:K] = times(other, couple[half]).astype(BF)

    pl.semaphore_wait(barrier, 67)

    started = []

    def send(src, dst, ssem, rsem, who):
        copy = pltpu.make_async_remote_copy(
            src_ref=src, dst_ref=dst, send_sem=ssem, recv_sem=rsem, device_id=who, device_id_type=MESH
        )
        copy.start()
        started.append(copy)
        return copy

    def trade(k):
        peer = lax.rem(s + k, 64)
        return pltpu.make_async_remote_copy(
            src_ref=tests.at[:, pl.ds(pl.multiple_of(peer * 768, 768), 768)],
            dst_ref=adj_in.at[s],
            send_sem=a2a_s,
            recv_sem=a2a_r,
            device_id={"sub": peer},
            device_id_type=MESH,
        )

    got_orders = [None, None]
    for i, who in ((0, right), (1, left)):
        got_orders[i] = send(leaf_perms.at[0], orders.at[i], near_ss.at[i], near_rs.at[i], {"sub": who})
    got_mate = send(omega, om_mate, near_ss.at[2], near_rs.at[2], {"sub": mate})

    def trade_start(k, carry):
        trade(k).start()
        return carry

    lax.fori_loop(1, 64, trade_start, 0)

    def cols(which):
        return pl.ds(pl.multiple_of(which * 128, 128), 128)

    got_lperm.wait()
    lrows[...] = jnp.zeros_like(lrows)
    lrows[0:2] = lperm[...].astype(F32)
    lcols = lrows[...].T
    base = ((g * 64 + s) - 1) * 6
    got_near.wait()

    def place(q, carry):
        held = [tile_cols[q, t] - base for t in range(12)]
        for m in range(18):
            at = 0
            for t in range(12):
                at = jnp.where(held[t] == m, t + 1, at)
            tile = near[q, jnp.maximum(at - 1, 0)]
            keep = jnp.where(at > 0, 1.0, 0.0)
            placed[pl.ds(pl.multiple_of(q * 128, 128), 128), m * 128 : (m + 1) * 128] = tile * keep.astype(BF)
        return carry

    lax.fori_loop(0, 6, place, 0)
    picked = onehot(lcols[0:K, 0:1], 768).astype(BF)
    for k in range(3):
        wf[k] = mm(picked, placed[:, k * 768 : (k + 1) * 768]).astype(BF)
    got_w = send(wf.at[2 * core], w_in, near_ss.at[3], near_rs.at[3], {"sub": outer})

    firsts = [None] * 5

    def first(q, value):
        s0[q] = value.astype(BF)
        firsts[q] = send(s0.at[q], r0.at[q], ss0.at[q], rs0.at[q], {"sub": mate})

    def outward(i, value):
        for half in range(2):
            d_s[i, half] = value[:, half * 128 : half * 128 + 128].astype(BF)
        copies = []
        for n, (half, who) in enumerate(((1 - core, outer), (core, outer_twin))):
            copies.append(
                send(d_s.at[i, half], d_r.at[i, 1 - core], d_ss.at[i, n], d_rs.at[i, 1 - core], {"sub": who})
            )
        return copies

    def outward_done(i):
        for slot in range(2):
            pltpu.make_async_remote_copy(
                src_ref=d_s.at[i, slot],
                dst_ref=d_r.at[i, slot],
                send_sem=d_ss.at[i, slot],
                recv_sem=d_rs.at[i, slot],
                device_id={"sub": outer},
                device_id_type=MESH,
            ).wait_recv()

    got_interp.wait()
    for i in (1, 0):
        into = gl if i == 1 else wa
        tail = onehot(lcols[K:768, i : i + 1], 768).astype(BF)
        into[1] = (onehot(lcols[0:K, i : i + 1], 768) + mm(interp[i], tail)).astype(BF)
    got_om.wait()
    pan[1] = mm(gl[1], om[...])
    first(1, pan[1, :, cols(1 - core)])
    got_mate.wait_recv()
    pan[0] = mm(wf[1], om[...]) + mm(wf[2 * (1 - core)], om_mate[...])
    first(0, pan[0, :, cols(1 - core)])
    erows[...] = jnp.zeros_like(erows)
    for i in range(2):
        got_orders[i].wait_recv()
        erows[i : i + 1] = orders[i, 1:2, 0:128].astype(F32)
    ecols = erows[...].T
    for k, col in enumerate((ecols[0:K, 0:1], lcols[0:K, 1:2], ecols[0:K, 1:2])):
        at = (3 * core, 2, 3 * (1 - core))[k]
        wa[at] = mm_nt(onehot(col, 768).astype(BF), placed[:, k * 768 : (k + 1) * 768]).astype(BF)
    got_w.wait_recv()
    outward(0, mm(w_in[...], om[...]))

    def chain_send(ch, i):
        return pltpu.make_async_remote_copy(
            src_ref=hi.at[0, 2 * ch + i],
            dst_ref=rec.at[0, i],
            send_sem=ss.at[0, i],
            recv_sem=rs.at[0, i],
            device_id=partners[1],
            device_id_type=MESH,
        )

    def chain_start(ch, i):
        @pl.when(z0 == 1 - ch)
        def _():
            chain_send(ch, i).start()

    def tests_up(ch):
        own, far = ch * 2 + core, ch * 2 + 1 - core
        q = 2 * ch + 1
        top, low = split(pan[q, :, cols(core)])
        firsts[q].wait_recv()
        top_new, lo[q] = split(twice(op_g[own][:, :K], top, low) + mm(op_g[far][:, :K], r0[q]))
        hi[0, q] = top_new
        chain_start(ch, 1)
        return twice(op_h[own][:, :K], top, low) + mm(op_h[far][:, :K], r0[q])

    def rows_up(ch, coupled, own_rows, far_rows):
        own, far = ch * 2 + core, ch * 2 + 1 - core
        new = twice(op_s[own][:, :K], *split(own_rows)) + twice(op_s[far][:, :K], *split(far_rows)) - coupled
        top_new, lo[2 * ch] = split(new)
        hi[0, 2 * ch] = top_new
        chain_start(ch, 0)
        out[0, ch, :, cols(core)] = top_new
        arrivals.append(
            send(hi.at[0, 2 * ch], out.at[0, ch, :, cols(core)], os_s.at[0, ch], os_r.at[0, ch], partners[0])
        )

    arrivals = []
    coupled_fwd = tests_up(0)

    own_tests.wait()
    everyone = adj_in.at[pl.ds(0, 63)]
    trades = pltpu.make_async_remote_copy(
        src_ref=everyone,
        dst_ref=everyone,
        send_sem=a2a_s,
        recv_sem=a2a_r,
        device_id={"sub": right},
        device_id_type=MESH,
    )
    trades.wait_recv()
    adj[...] = adj_in[...].reshape(256, 768)
    outward(1, mm_nt(wa[0], adj[...]))
    inner = mm_nt(wa[1:4].reshape(3 * K, 768), adj[...])
    pan[3] = inner[0:K]
    pan[2] = inner[K : 2 * K]
    pan_far[...] = inner[2 * K :]
    first(3, pan[3, :, cols(1 - core)])
    first(4, pan[2, :, cols(1 - core)])
    first(2, pan_far[:, cols(1 - core)])
    firsts[0].wait_recv()
    outward_done(0)
    rows_up(
        0,
        coupled_fwd,
        pan[0, :, cols(core)] + d_r[0, core].astype(F32),
        r0[0].astype(F32) + d_r[0, 1 - core].astype(F32),
    )
    coupled_adj = tests_up(1)
    firsts[2].wait_recv()
    firsts[4].wait_recv()
    outward_done(1)
    rows_up(
        1,
        coupled_adj,
        pan[2, :, cols(core)] + r0[2].astype(F32) + d_r[1, core].astype(F32),
        pan_far[:, cols(core)] + r0[4].astype(F32) + d_r[1, 1 - core].astype(F32),
    )
    ways = [chain_send(0, 0), chain_send(0, 1)]
    started += ways
    f_top, o_top = hi[0, 2 * z0], hi[0, 2 * z0 + 1]
    f_low, o_low = lo[2 * z0], lo[2 * z0 + 1]
    peers = ({"sub": mate}, {"sub": zmate}, {"sub": cross})
    def publish(j, top=None):
        if top is not None:
            hi[j, 0] = top
            out[j, z0, :, cols(core)] = top
        for k, who in enumerate(peers):
            arrivals.append(
                send(hi.at[j, 0], out.at[j, z0, :, cols(core)], os_s.at[j, k], os_r.at[j, k], who)
            )

    last = LEVELS - 3
    for j in range(1, last + 1):
        base = (j * 2 + z0) * 2
        own, far = base + bits[j], base + 1 - bits[j]
        o_part = twice(op_g[own][:, :K], o_top, o_low)
        f_part = twice(op_s[own][:, :K], f_top, f_low) - twice(op_h[own][:, :K], o_top, o_low)
        ways[1].wait_recv()
        o_far = rec[j - 1, 1]
        nexts = [None, None]
        o_top, o_low = split(o_part + mm(op_g[far][:, :K], o_far))
        if j < last:
            hi[j, 1] = o_top
            nexts[1] = send(hi.at[j, 1], rec.at[j, 1], ss.at[j, 1], rs.at[j, 1], partners[j + 1])
        f_part = f_part - mm(op_h[far][:, :K], o_far)
        ways[0].wait_recv()
        f_top, f_low = split(f_part + mm(op_s[far][:, :K], rec[j - 1, 0]))
        if j < last:
            hi[j, 0] = f_top
            nexts[0] = send(hi.at[j, 0], rec.at[j, 0], ss.at[j, 0], rs.at[j, 0], partners[j + 1])
            out[j, z0, :, cols(core)] = f_top
            for due in {3: (1, 2), 4: (3, 4), 5: (5,)}.get(j, ()):
                publish(due)
        ways = nexts

    a = ((LEVELS - 2) * 2 + z0) * 2 + bits[LEVELS - 2]
    b = ((LEVELS - 1) * 2 + z0) * 2 + bits[LEVELS - 1]
    o_seven = twice(op_g[a][:, :K], o_top, o_low)
    h_eight = twice(op_h[b][:, :K], *split(o_seven))
    f_seven = twice(op_s[a][:, :K], f_top, f_low) - twice(op_h[a][:, :K], o_top, o_low)
    fin_s[1] = f_seven.astype(BF)
    got_seven = send(fin_s.at[1], fin_r.at[3], fin_ss.at[3], fin_rs.at[3], partners[7])
    f_eight = twice(op_s[b][:, :K], *split(f_seven)) - h_eight
    fin_s[0] = f_eight.astype(BF)
    got_eight = []
    for k, who in ((1, partners[9]), (2, partners[8]), (0, partners[7])):
        got_eight.append(send(fin_s.at[0], fin_r.at[k], fin_ss.at[k], fin_rs.at[k], who))
    publish(last, f_top)
    got_seven.wait_recv()
    publish(LEVELS - 2, (f_seven + fin_r[3].astype(F32)).astype(BF))
    for copy in got_eight:
        copy.wait_recv()
    for k in range(3):
        f_eight = f_eight + fin_r[k].astype(F32)
    publish(LEVELS - 1, f_eight.astype(BF))
    for copy in arrivals:
        copy.wait_recv()
    for copy in started:
        copy.wait_send()

    trades.wait_send()


def local(omega, adj_tests, near_tiles, tile_cols, leaf_perms, leaf_interp, node_perms, node_maps):
    dma = pltpu.SemaphoreType.DMA
    anywhere = pl.BlockSpec(memory_space=pl.ANY)
    ops = pltpu.VMEM((LEVELS * 4, K, 128), BF)
    return pl.pallas_call(
        kernel,
        out_shape=jax.ShapeDtypeStruct((LEVELS, 2, K, 256), BF),
        in_specs=[pl.BlockSpec(memory_space=pltpu.SMEM)] + [anywhere] * 7,
        out_specs=pl.BlockSpec(memory_space=pltpu.VMEM),
        scratch_shapes=[
            pltpu.VMEM((768, 256), BF),
            pltpu.VMEM((768, 256), BF),
            pltpu.VMEM((K, 768), BF),
            pltpu.VMEM((6, 12, 128, 128), BF),
            pltpu.VMEM((2, 768), jnp.int32),
            pltpu.VMEM((2, K, 672), BF),
            pltpu.VMEM((LEVELS, 2, 192), jnp.int32),
            pltpu.VMEM((LEVELS, 4, K, K), BF),
            pltpu.VMEM((24, 256), F32),
            pltpu.VMEM((8, 768), F32),
            pltpu.VMEM((8, 128), F32),
            pltpu.VMEM((2, 2, 768), jnp.int32),
            pltpu.VMEM((768, 2304), BF),
            pltpu.VMEM((3, K, 768), BF),
            pltpu.VMEM((4, K, 768), BF),
            pltpu.VMEM((2, K, 768), BF),
            ops,
            ops,
            ops,
            pltpu.VMEM((64, 4, 768), BF),
            pltpu.VMEM((256, 768), BF),
            pltpu.VMEM((4, K, 256), F32),
            pltpu.VMEM((K, 256), F32),
            pltpu.VMEM((2, 2, K, 128), BF),
            pltpu.VMEM((2, 2, K, 128), BF),
            pltpu.VMEM((5, K, 128), BF),
            pltpu.VMEM((5, K, 128), BF),
            pltpu.VMEM((LEVELS, 4, K, 128), BF),
            pltpu.VMEM((4, K, 128), BF),
            pltpu.VMEM((LEVELS - 1, 2, K, 128), BF),
            pltpu.VMEM((2, K, 128), BF),
            pltpu.VMEM((4, K, 128), BF),
            dma((7,)),
            dma,
            dma,
            dma((4,)),
            dma((4,)),
            dma((2, 2)),
            dma((2, 2)),
            dma((5,)),
            dma((5,)),
            dma((LEVELS, 2)),
            dma((LEVELS, 2)),
            dma((LEVELS, 3)),
            dma((LEVELS, 3)),
            dma((4,)),
            dma((4,)),
        ],
        compiler_params=pltpu.CompilerParams(
            collective_id=0, has_side_effects=True, vmem_limit_bytes=28 << 20
        ),
        name="window",
    )(
        *(
            pltpu.with_memory_space_constraint(x, pltpu.HBM)
            for x in (
                tile_cols,
                omega,
                adj_tests,
                near_tiles,
                leaf_perms,
                jnp.swapaxes(leaf_interp, 2, 3),
                node_perms,
                node_maps,
            )
        ),
    )[None]


def solution(mesh):
    placed = (
        P(("grp", "sub"), None),
        P("sub", "grp"),
        P(("grp", "sub"), None, None, None),
        P(("grp", "sub"), None),
        P(("grp", "sub"), None, None),
        P(("grp", "sub"), None, None, None),
        P(("grp", "sub"), None, None, None),
        P(("grp", "sub"), None, None, None, None),
    )
    return jax.shard_map(
        local,
        mesh=mesh,
        in_specs=placed,
        out_specs=P(("grp", "sub"), None, None, None, None),
        check_vma=False,
    )
```

```python
import jax
import jax.numpy as jnp
from jax import lax
from jax.experimental import pallas as pl
from jax.experimental.pallas import tpu as pltpu
from jax.sharding import PartitionSpec as P

BF = jnp.bfloat16
F32 = jnp.float32
MESH = pl.DeviceIdType.MESH
K = 96
LEVELS = 9


def mm(a, b):
    return lax.dot_general(a, b, (((1,), (0,)), ((), ())), preferred_element_type=F32)


def mm_nt(a, b):
    return lax.dot_general(a, b, (((1,), (1,)), ((), ())), preferred_element_type=F32)


def mm_tn(a, b):
    return lax.dot_general(a, b, (((0,), (0,)), ((), ())), preferred_element_type=F32)


def onehot(column, width):
    lanes = lax.broadcasted_iota(jnp.int32, (column.shape[0], width), 1).astype(F32)
    return jnp.where(lanes == column, 1.0, 0.0)


def mirror(z):
    return lax.rem(jnp.where(lax.rem(z, 2) == 0, 14 - z, 16 - z), 8)


def flip(v, bit):
    return jnp.where(lax.rem(v // bit, 2) == 0, v + bit, v - bit)


def split(value):
    top = value.astype(BF)
    return top, (value - top.astype(F32)).astype(BF)


def twice(op, top, low):
    return mm(op, top) + mm(op, low)


def kernel(
    tile_cols, omega, tests, near_in, leaf_perms, interp_in, node_perms, maps_in,
    out,
    om, om_mate, w_in, near, lperm, interp, nperm, maps, nrows, lrows, erows, orders, placed, wf, wa, gl, op_s, op_h, op_g,
    adj_in, adj, pan, pan_far, d_s, d_r, s0, r0, hi, lo, rec, fin_s, fin_r,
    loc, a2a_s, a2a_r, near_ss, near_rs, d_ss, d_rs, ss0, rs0, ss, rs, os_s, os_r, fin_ss, fin_rs,
):
    g = lax.axis_index("grp")
    s = lax.axis_index("sub")
    core = lax.rem(s, 2)
    z = lax.rem(s // 2, 8)
    x = s // 16
    z0 = lax.rem(z, 2)
    left, right = lax.rem(s + 63, 64), lax.rem(s + 1, 64)
    outer = lax.rem(s + 63 + 2 * core, 64)
    outer_twin = lax.rem(s + 62 + 4 * core, 64)

    def sub_at(xx, zz, cc):
        return (xx * 8 + zz) * 2 + cc

    mate = sub_at(x, z, 1 - core)
    zmate = sub_at(x, flip(z, 1), core)
    cross = sub_at(x, flip(z, 1), 1 - core)
    partners = [
        {"sub": mate},
        {"sub": zmate},
        {"sub": sub_at(x, flip(z, 2), core)},
        {"sub": sub_at(x, mirror(z), core)},
        {"sub": sub_at(flip(x, 1), z, core)},
        {"sub": sub_at(3 - x, z, core)},
        {"grp": flip(g, 1)},
        {"grp": flip(g, 2)},
        {"grp": mirror(g)},
        {"grp": jnp.where(lax.rem(g // 2, 2) == 0, 5 - g, 9 - g)},
    ]
    bits = [core] + [lax.rem(z // b, 2) for b in (1, 2, 4)] + [lax.rem(x // b, 2) for b in (1, 2)]
    bits += [lax.rem(g // b, 2) for b in (1, 2, 4)]

    barrier = pltpu.get_barrier_semaphore()

    def greet(k, carry):
        pl.semaphore_signal(
            barrier, inc=1, device_id={"sub": lax.rem(s + k, 64)}, device_id_type=MESH
        )
        return carry

    lax.fori_loop(1, 64, greet, 0)
    for who in partners[6:]:
        pl.semaphore_signal(barrier, inc=1, device_id=who, device_id_type=MESH)

    def fetch(src, dst, i):
        copy = pltpu.make_async_copy(src, dst, loc.at[i])
        copy.start()
        return copy

    got_nperm = fetch(node_perms.at[0], nperm, 0)
    got_maps = fetch(maps_in.at[0], maps, 1)
    got_lperm = fetch(leaf_perms.at[0], lperm, 2)
    got_near = fetch(near_in, near, 3)
    got_interp = fetch(interp_in.at[0], interp, 4)
    got_om = fetch(omega, om, 5)
    own_tests = fetch(tests.at[:, pl.ds(pl.multiple_of(s * 768, 768), 768)], adj_in.at[s], 6)

    got_nperm.wait()
    nrows[...] = jnp.zeros_like(nrows)
    for j in range(LEVELS):
        nrows[2 * j : 2 * j + 2, 0:192] = nperm[j].astype(F32)
    ncols = nrows[...].T
    ncols = ncols + jnp.where(ncols >= K, 128.0 - K, 0.0)
    got_maps.wait()
    for j in range(LEVELS):
        picks = [onehot(ncols[0:192, 2 * j + i : 2 * j + i + 1], 256) for i in range(2)]
        low_high, high_low = maps[j, 2], maps[j, 3]
        for ch in range(2):
            sel = picks[ch][:K].astype(BF)
            rows = picks[1 - ch]
            full = (rows[:K] + mm_tn(maps[j, 1 - ch], rows[K:].astype(BF))).astype(BF)
            couple = (high_low, low_high) if ch == 0 else (low_high, high_low)
            times = mm if ch == 0 else mm_nt
            for half in range(2):
                at = (j * 2 + ch) * 2 + half
                op_s[at] = sel[:, half * 128 : half * 128 + 128]
                op_g[at] = full[:, half * 128 : half * 128 + 128]
                other = sel[:, (1 - half) * 128 : (1 - half) * 128 + K]
                op_h[at, :, 0:K] = times(other, couple[half]).astype(BF)

    pl.semaphore_wait(barrier, 67)

    started = []

    def send(src, dst, ssem, rsem, who):
        copy = pltpu.make_async_remote_copy(
            src_ref=src, dst_ref=dst, send_sem=ssem, recv_sem=rsem, device_id=who, device_id_type=MESH
        )
        copy.start()
        started.append(copy)
        return copy

    def trade(k):
        peer = lax.rem(s + k, 64)
        return pltpu.make_async_remote_copy(
            src_ref=tests.at[:, pl.ds(pl.multiple_of(peer * 768, 768), 768)],
            dst_ref=adj_in.at[s],
            send_sem=a2a_s,
            recv_sem=a2a_r,
            device_id={"sub": peer},
            device_id_type=MESH,
        )

    got_orders = [None, None]
    for i, who in ((0, right), (1, left)):
        got_orders[i] = send(leaf_perms.at[0], orders.at[i], near_ss.at[i], near_rs.at[i], {"sub": who})
    got_mate = send(omega, om_mate, near_ss.at[2], near_rs.at[2], {"sub": mate})

    def trade_start(k, carry):
        trade(k).start()
        return carry

    lax.fori_loop(1, 64, trade_start, 0)

    def cols(which):
        return pl.ds(pl.multiple_of(which * 128, 128), 128)

    got_lperm.wait()
    lrows[...] = jnp.zeros_like(lrows)
    lrows[0:2] = lperm[...].astype(F32)
    lcols = lrows[...].T
    base = ((g * 64 + s) - 1) * 6
    got_near.wait()

    def place(q, carry):
        held = [tile_cols[q, t] - base for t in range(12)]
        for m in range(18):
            at = 0
            for t in range(12):
                at = jnp.where(held[t] == m, t + 1, at)
            tile = near[q, jnp.maximum(at - 1, 0)]
            keep = jnp.where(at > 0, 1.0, 0.0)
            placed[pl.ds(pl.multiple_of(q * 128, 128), 128), m * 128 : (m + 1) * 128] = tile * keep.astype(BF)
        return carry

    lax.fori_loop(0, 6, place, 0)
    picked = onehot(lcols[0:K, 0:1], 768).astype(BF)
    for k in range(3):
        wf[k] = mm(picked, placed[:, k * 768 : (k + 1) * 768]).astype(BF)
    got_w = send(wf.at[2 * core], w_in, near_ss.at[3], near_rs.at[3], {"sub": outer})

    firsts = [None] * 5

    def first(q, value):
        s0[q] = value.astype(BF)
        firsts[q] = send(s0.at[q], r0.at[q], ss0.at[q], rs0.at[q], {"sub": mate})

    def outward(i, value):
        for half in range(2):
            d_s[i, half] = value[:, half * 128 : half * 128 + 128].astype(BF)
        copies = []
        for n, (half, who) in enumerate(((1 - core, outer), (core, outer_twin))):
            copies.append(
                send(d_s.at[i, half], d_r.at[i, 1 - core], d_ss.at[i, n], d_rs.at[i, 1 - core], {"sub": who})
            )
        return copies

    def outward_done(i):
        for slot in range(2):
            pltpu.make_async_remote_copy(
                src_ref=d_s.at[i, slot],
                dst_ref=d_r.at[i, slot],
                send_sem=d_ss.at[i, slot],
                recv_sem=d_rs.at[i, slot],
                device_id={"sub": outer},
                device_id_type=MESH,
            ).wait_recv()

    got_interp.wait()
    for i in (1, 0):
        into = gl if i == 1 else wa
        tail = onehot(lcols[K:768, i : i + 1], 768).astype(BF)
        into[1] = (onehot(lcols[0:K, i : i + 1], 768) + mm(interp[i], tail)).astype(BF)
    got_om.wait()
    pan[1] = mm(gl[1], om[...])
    first(1, pan[1, :, cols(1 - core)])
    got_mate.wait_recv()
    pan[0] = mm(wf[1], om[...]) + mm(wf[2 * (1 - core)], om_mate[...])
    first(0, pan[0, :, cols(1 - core)])
    erows[...] = jnp.zeros_like(erows)
    for i in range(2):
        got_orders[i].wait_recv()
        erows[i : i + 1] = orders[i, 1:2, 0:128].astype(F32)
    ecols = erows[...].T
    for k, col in enumerate((ecols[0:K, 0:1], lcols[0:K, 1:2], ecols[0:K, 1:2])):
        at = (3 * core, 2, 3 * (1 - core))[k]
        wa[at] = mm_nt(onehot(col, 768).astype(BF), placed[:, k * 768 : (k + 1) * 768]).astype(BF)
    got_w.wait_recv()
    outward(0, mm(w_in[...], om[...]))

    def chain_send(ch, i):
        return pltpu.make_async_remote_copy(
            src_ref=hi.at[0, 2 * ch + i],
            dst_ref=rec.at[0, i],
            send_sem=ss.at[0, i],
            recv_sem=rs.at[0, i],
            device_id=partners[1],
            device_id_type=MESH,
        )

    def chain_start(ch, i):
        @pl.when(z0 == 1 - ch)
        def _():
            chain_send(ch, i).start()

    def tests_up(ch):
        own, far = ch * 2 + core, ch * 2 + 1 - core
        q = 2 * ch + 1
        top, low = split(pan[q, :, cols(core)])
        firsts[q].wait_recv()
        top_new, lo[q] = split(twice(op_g[own][:, :K], top, low) + mm(op_g[far][:, :K], r0[q]))
        hi[0, q] = top_new
        chain_start(ch, 1)
        return twice(op_h[own][:, :K], top, low) + mm(op_h[far][:, :K], r0[q])

    def rows_up(ch, coupled, own_rows, far_rows):
        own, far = ch * 2 + core, ch * 2 + 1 - core
        new = twice(op_s[own][:, :K], *split(own_rows)) + twice(op_s[far][:, :K], *split(far_rows)) - coupled
        top_new, lo[2 * ch] = split(new)
        hi[0, 2 * ch] = top_new
        chain_start(ch, 0)
        out[0, ch, :, cols(core)] = top_new
        arrivals.append(
            send(hi.at[0, 2 * ch], out.at[0, ch, :, cols(core)], os_s.at[0, ch], os_r.at[0, ch], partners[0])
        )

    arrivals = []
    coupled_fwd = tests_up(0)

    own_tests.wait()
    everyone = adj_in.at[pl.ds(0, 63)]
    trades = pltpu.make_async_remote_copy(
        src_ref=everyone,
        dst_ref=everyone,
        send_sem=a2a_s,
        recv_sem=a2a_r,
        device_id={"sub": right},
        device_id_type=MESH,
    )
    trades.wait_recv()
    adj[...] = adj_in[...].reshape(256, 768)
    outward(1, mm_nt(wa[0], adj[...]))
    inner = mm_nt(wa[1:4].reshape(3 * K, 768), adj[...])
    pan[3] = inner[0:K]
    pan[2] = inner[K : 2 * K]
    pan_far[...] = inner[2 * K :]
    first(3, pan[3, :, cols(1 - core)])
    first(4, pan[2, :, cols(1 - core)])
    first(2, pan_far[:, cols(1 - core)])
    firsts[0].wait_recv()
    outward_done(0)
    rows_up(
        0,
        coupled_fwd,
        pan[0, :, cols(core)] + d_r[0, core].astype(F32),
        r0[0].astype(F32) + d_r[0, 1 - core].astype(F32),
    )
    coupled_adj = tests_up(1)
    firsts[2].wait_recv()
    firsts[4].wait_recv()
    outward_done(1)
    rows_up(
        1,
        coupled_adj,
        pan[2, :, cols(core)] + r0[2].astype(F32) + d_r[1, core].astype(F32),
        pan_far[:, cols(core)] + r0[4].astype(F32) + d_r[1, 1 - core].astype(F32),
    )
    ways = [chain_send(0, 0), chain_send(0, 1)]
    started += ways
    f_top, o_top = hi[0, 2 * z0], hi[0, 2 * z0 + 1]
    f_low, o_low = lo[2 * z0], lo[2 * z0 + 1]
    peers = ({"sub": mate}, {"sub": zmate}, {"sub": cross})
    def publish(j, top=None):
        if top is not None:
            hi[j, 0] = top
            out[j, z0, :, cols(core)] = top
        for k, who in enumerate(peers):
            arrivals.append(
                send(hi.at[j, 0], out.at[j, z0, :, cols(core)], os_s.at[j, k], os_r.at[j, k], who)
            )

    last = LEVELS - 3
    for j in range(1, last + 1):
        base = (j * 2 + z0) * 2
        own, far = base + bits[j], base + 1 - bits[j]
        o_part = twice(op_g[own][:, :K], o_top, o_low)
        f_part = twice(op_s[own][:, :K], f_top, f_low) - twice(op_h[own][:, :K], o_top, o_low)
        ways[1].wait_recv()
        o_far = rec[j - 1, 1]
        nexts = [None, None]
        o_top, o_low = split(o_part + mm(op_g[far][:, :K], o_far))
        if j < last:
            hi[j, 1] = o_top
            nexts[1] = send(hi.at[j, 1], rec.at[j, 1], ss.at[j, 1], rs.at[j, 1], partners[j + 1])
        f_part = f_part - mm(op_h[far][:, :K], o_far)
        ways[0].wait_recv()
        f_top, f_low = split(f_part + mm(op_s[far][:, :K], rec[j - 1, 0]))
        if j < last:
            hi[j, 0] = f_top
            nexts[0] = send(hi.at[j, 0], rec.at[j, 0], ss.at[j, 0], rs.at[j, 0], partners[j + 1])
            out[j, z0, :, cols(core)] = f_top
            for due in {3: (1, 2), 4: (3, 4), 5: (5,)}.get(j, ()):
                publish(due)
        ways = nexts

    a = ((LEVELS - 2) * 2 + z0) * 2 + bits[LEVELS - 2]
    b = ((LEVELS - 1) * 2 + z0) * 2 + bits[LEVELS - 1]
    o_seven = twice(op_g[a][:, :K], o_top, o_low)
    h_eight = twice(op_h[b][:, :K], *split(o_seven))
    f_seven = twice(op_s[a][:, :K], f_top, f_low) - twice(op_h[a][:, :K], o_top, o_low)
    fin_s[1] = f_seven.astype(BF)
    f_eight = twice(op_s[b][:, :K], *split(f_seven)) - h_eight
    fin_s[0] = f_eight.astype(BF)
    got_eight = []
    for k, who in ((1, partners[9]), (2, partners[8]), (0, partners[7])):
        got_eight.append(send(fin_s.at[0], fin_r.at[k], fin_ss.at[k], fin_rs.at[k], who))
    got_seven = send(fin_s.at[1], fin_r.at[3], fin_ss.at[3], fin_rs.at[3], partners[7])
    publish(last, f_top)
    got_seven.wait_recv()
    publish(LEVELS - 2, (f_seven + fin_r[3].astype(F32)).astype(BF))
    for copy in got_eight:
        copy.wait_recv()
    for k in range(3):
        f_eight = f_eight + fin_r[k].astype(F32)
    publish(LEVELS - 1, f_eight.astype(BF))
    for copy in arrivals:
        copy.wait_recv()
    for copy in started:
        copy.wait_send()

    trades.wait_send()


def local(omega, adj_tests, near_tiles, tile_cols, leaf_perms, leaf_interp, node_perms, node_maps):
    dma = pltpu.SemaphoreType.DMA
    anywhere = pl.BlockSpec(memory_space=pl.ANY)
    ops = pltpu.VMEM((LEVELS * 4, K, 128), BF)
    return pl.pallas_call(
        kernel,
        out_shape=jax.ShapeDtypeStruct((LEVELS, 2, K, 256), BF),
        in_specs=[pl.BlockSpec(memory_space=pltpu.SMEM)] + [anywhere] * 7,
        out_specs=pl.BlockSpec(memory_space=pltpu.VMEM),
        scratch_shapes=[
            pltpu.VMEM((768, 256), BF),
            pltpu.VMEM((768, 256), BF),
            pltpu.VMEM((K, 768), BF),
            pltpu.VMEM((6, 12, 128, 128), BF),
            pltpu.VMEM((2, 768), jnp.int32),
            pltpu.VMEM((2, K, 672), BF),
            pltpu.VMEM((LEVELS, 2, 192), jnp.int32),
            pltpu.VMEM((LEVELS, 4, K, K), BF),
            pltpu.VMEM((24, 256), F32),
            pltpu.VMEM((8, 768), F32),
            pltpu.VMEM((8, 128), F32),
            pltpu.VMEM((2, 2, 768), jnp.int32),
            pltpu.VMEM((768, 2304), BF),
            pltpu.VMEM((3, K, 768), BF),
            pltpu.VMEM((4, K, 768), BF),
            pltpu.VMEM((2, K, 768), BF),
            ops,
            ops,
            ops,
            pltpu.VMEM((64, 4, 768), BF),
            pltpu.VMEM((256, 768), BF),
            pltpu.VMEM((4, K, 256), F32),
            pltpu.VMEM((K, 256), F32),
            pltpu.VMEM((2, 2, K, 128), BF),
            pltpu.VMEM((2, 2, K, 128), BF),
            pltpu.VMEM((5, K, 128), BF),
            pltpu.VMEM((5, K, 128), BF),
            pltpu.VMEM((LEVELS, 4, K, 128), BF),
            pltpu.VMEM((4, K, 128), BF),
            pltpu.VMEM((LEVELS - 1, 2, K, 128), BF),
            pltpu.VMEM((2, K, 128), BF),
            pltpu.VMEM((4, K, 128), BF),
            dma((7,)),
            dma,
            dma,
            dma((4,)),
            dma((4,)),
            dma((2, 2)),
            dma((2, 2)),
            dma((5,)),
            dma((5,)),
            dma((LEVELS, 2)),
            dma((LEVELS, 2)),
            dma((LEVELS, 3)),
            dma((LEVELS, 3)),
            dma((4,)),
            dma((4,)),
        ],
        compiler_params=pltpu.CompilerParams(
            collective_id=0, has_side_effects=True, vmem_limit_bytes=28 << 20
        ),
        name="window",
    )(
        *(
            pltpu.with_memory_space_constraint(x, pltpu.HBM)
            for x in (
                tile_cols,
                omega,
                adj_tests,
                near_tiles,
                leaf_perms,
                jnp.swapaxes(leaf_interp, 2, 3),
                node_perms,
                node_maps,
            )
        ),
    )[None]


def solution(mesh):
    placed = (
        P(("grp", "sub"), None),
        P("sub", "grp"),
        P(("grp", "sub"), None, None, None),
        P(("grp", "sub"), None),
        P(("grp", "sub"), None, None),
        P(("grp", "sub"), None, None, None),
        P(("grp", "sub"), None, None, None),
        P(("grp", "sub"), None, None, None, None),
    )
    return jax.shard_map(
        local,
        mesh=mesh,
        in_specs=placed,
        out_specs=P(("grp", "sub"), None, None, None, None),
        check_vma=False,
    )
```

```python
import jax
import jax.numpy as jnp
from jax import lax
from jax.experimental import pallas as pl
from jax.experimental.pallas import tpu as pltpu
from jax.sharding import PartitionSpec as P

BF = jnp.bfloat16
F32 = jnp.float32
MESH = pl.DeviceIdType.MESH
K = 96
LEVELS = 9


def mm(a, b):
    return lax.dot_general(a, b, (((1,), (0,)), ((), ())), preferred_element_type=F32)


def mm_nt(a, b):
    return lax.dot_general(a, b, (((1,), (1,)), ((), ())), preferred_element_type=F32)


def mm_tn(a, b):
    return lax.dot_general(a, b, (((0,), (0,)), ((), ())), preferred_element_type=F32)


def onehot(column, width):
    lanes = lax.broadcasted_iota(jnp.int32, (column.shape[0], width), 1).astype(F32)
    return jnp.where(lanes == column, 1.0, 0.0)


def mirror(z):
    return lax.rem(jnp.where(lax.rem(z, 2) == 0, 14 - z, 16 - z), 8)


def flip(v, bit):
    return jnp.where(lax.rem(v // bit, 2) == 0, v + bit, v - bit)


def split(value):
    top = value.astype(BF)
    return top, (value - top.astype(F32)).astype(BF)


def twice(op, top, low):
    return mm(op, top) + mm(op, low)


def kernel(
    tile_cols, omega, tests, near_in, leaf_perms, interp_in, node_perms, maps_in,
    out,
    om, om_mate, w_in, near, lperm, interp, nperm, maps, nrows, lrows, erows, orders, placed, wf, wa, gl, op_s, op_h, op_g,
    adj_in, adj, pan, pan_far, d_s, d_r, s0, r0, hi, lo, rec, fin_s, fin_r,
    loc, a2a_s, a2a_r, near_ss, near_rs, d_ss, d_rs, ss0, rs0, ss, rs, os_s, os_r, fin_ss, fin_rs,
):
    g = lax.axis_index("grp")
    s = lax.axis_index("sub")
    core = lax.rem(s, 2)
    z = lax.rem(s // 2, 8)
    x = s // 16
    z0 = lax.rem(z, 2)
    left, right = lax.rem(s + 63, 64), lax.rem(s + 1, 64)
    outer = lax.rem(s + 63 + 2 * core, 64)
    outer_twin = lax.rem(s + 62 + 4 * core, 64)

    def sub_at(xx, zz, cc):
        return (xx * 8 + zz) * 2 + cc

    mate = sub_at(x, z, 1 - core)
    zmate = sub_at(x, flip(z, 1), core)
    cross = sub_at(x, flip(z, 1), 1 - core)
    partners = [
        {"sub": mate},
        {"sub": zmate},
        {"sub": sub_at(x, flip(z, 2), core)},
        {"sub": sub_at(x, mirror(z), core)},
        {"sub": sub_at(flip(x, 1), z, core)},
        {"sub": sub_at(3 - x, z, core)},
        {"grp": flip(g, 1)},
        {"grp": flip(g, 2)},
        {"grp": mirror(g)},
        {"grp": jnp.where(lax.rem(g // 2, 2) == 0, 5 - g, 9 - g)},
    ]
    bits = [core] + [lax.rem(z // b, 2) for b in (1, 2, 4)] + [lax.rem(x // b, 2) for b in (1, 2)]
    bits += [lax.rem(g // b, 2) for b in (1, 2, 4)]

    barrier = pltpu.get_barrier_semaphore()

    def greet(k, carry):
        pl.semaphore_signal(
            barrier, inc=1, device_id={"sub": lax.rem(s + k, 64)}, device_id_type=MESH
        )
        return carry

    lax.fori_loop(1, 64, greet, 0)
    for who in partners[6:]:
        pl.semaphore_signal(barrier, inc=1, device_id=who, device_id_type=MESH)

    def fetch(src, dst, i):
        copy = pltpu.make_async_copy(src, dst, loc.at[i])
        copy.start()
        return copy

    got_nperm = fetch(node_perms.at[0], nperm, 0)
    got_maps = fetch(maps_in.at[0], maps, 1)
    got_lperm = fetch(leaf_perms.at[0], lperm, 2)
    got_near = fetch(near_in, near, 3)
    got_interp = fetch(interp_in.at[0], interp, 4)
    got_om = fetch(omega, om, 5)
    own_tests = fetch(tests.at[:, pl.ds(pl.multiple_of(s * 768, 768), 768)], adj_in.at[s], 6)

    got_nperm.wait()
    nrows[...] = jnp.zeros_like(nrows)
    for j in range(LEVELS):
        nrows[2 * j : 2 * j + 2, 0:192] = nperm[j].astype(F32)
    ncols = nrows[...].T
    ncols = ncols + jnp.where(ncols >= K, 128.0 - K, 0.0)
    got_maps.wait()
    for j in range(LEVELS):
        picks = [onehot(ncols[0:192, 2 * j + i : 2 * j + i + 1], 256) for i in range(2)]
        low_high, high_low = maps[j, 2], maps[j, 3]
        for ch in range(2):
            sel = picks[ch][:K].astype(BF)
            rows = picks[1 - ch]
            full = (rows[:K] + mm_tn(maps[j, 1 - ch], rows[K:].astype(BF))).astype(BF)
            couple = (high_low, low_high) if ch == 0 else (low_high, high_low)
            times = mm if ch == 0 else mm_nt
            for half in range(2):
                at = (j * 2 + ch) * 2 + half
                op_s[at] = sel[:, half * 128 : half * 128 + 128]
                op_g[at] = full[:, half * 128 : half * 128 + 128]
                other = sel[:, (1 - half) * 128 : (1 - half) * 128 + K]
                op_h[at, :, 0:K] = times(other, couple[half]).astype(BF)

    pl.semaphore_wait(barrier, 67)

    started = []

    def send(src, dst, ssem, rsem, who):
        copy = pltpu.make_async_remote_copy(
            src_ref=src, dst_ref=dst, send_sem=ssem, recv_sem=rsem, device_id=who, device_id_type=MESH
        )
        copy.start()
        started.append(copy)
        return copy

    def trade(k):
        peer = lax.rem(s + k, 64)
        return pltpu.make_async_remote_copy(
            src_ref=tests.at[:, pl.ds(pl.multiple_of(peer * 768, 768), 768)],
            dst_ref=adj_in.at[s],
            send_sem=a2a_s,
            recv_sem=a2a_r,
            device_id={"sub": peer},
            device_id_type=MESH,
        )

    got_orders = [None, None]
    for i, who in ((0, right), (1, left)):
        got_orders[i] = send(leaf_perms.at[0], orders.at[i], near_ss.at[i], near_rs.at[i], {"sub": who})
    got_mate = send(omega, om_mate, near_ss.at[2], near_rs.at[2], {"sub": mate})

    def trade_start(k, carry):
        trade(k).start()
        return carry

    lax.fori_loop(1, 64, trade_start, 0)

    def cols(which):
        return pl.ds(pl.multiple_of(which * 128, 128), 128)

    got_lperm.wait()
    lrows[...] = jnp.zeros_like(lrows)
    lrows[0:2] = lperm[...].astype(F32)
    lcols = lrows[...].T
    base = ((g * 64 + s) - 1) * 6
    got_near.wait()

    def place(q, carry):
        held = [tile_cols[q, t] - base for t in range(12)]
        for m in range(18):
            at = 0
            for t in range(12):
                at = jnp.where(held[t] == m, t + 1, at)
            tile = near[q, jnp.maximum(at - 1, 0)]
            keep = jnp.where(at > 0, 1.0, 0.0)
            placed[pl.ds(pl.multiple_of(q * 128, 128), 128), m * 128 : (m + 1) * 128] = tile * keep.astype(BF)
        return carry

    lax.fori_loop(0, 6, place, 0)
    picked = onehot(lcols[0:K, 0:1], 768).astype(BF)
    for k in range(3):
        wf[k] = mm(picked, placed[:, k * 768 : (k + 1) * 768]).astype(BF)
    got_w = send(wf.at[2 * core], w_in, near_ss.at[3], near_rs.at[3], {"sub": outer})

    firsts = [None] * 5

    def first(q, value):
        s0[q] = value.astype(BF)
        firsts[q] = send(s0.at[q], r0.at[q], ss0.at[q], rs0.at[q], {"sub": mate})

    def outward(i, value):
        for half in range(2):
            d_s[i, half] = value[:, half * 128 : half * 128 + 128].astype(BF)
        copies = []
        for n, (half, who) in enumerate(((1 - core, outer), (core, outer_twin))):
            copies.append(
                send(d_s.at[i, half], d_r.at[i, 1 - core], d_ss.at[i, n], d_rs.at[i, 1 - core], {"sub": who})
            )
        return copies

    def outward_done(i):
        for slot in range(2):
            pltpu.make_async_remote_copy(
                src_ref=d_s.at[i, slot],
                dst_ref=d_r.at[i, slot],
                send_sem=d_ss.at[i, slot],
                recv_sem=d_rs.at[i, slot],
                device_id={"sub": outer},
                device_id_type=MESH,
            ).wait_recv()

    got_interp.wait()
    for i in (1, 0):
        into = gl if i == 1 else wa
        tail = onehot(lcols[K:768, i : i + 1], 768).astype(BF)
        into[1] = (onehot(lcols[0:K, i : i + 1], 768) + mm(interp[i], tail)).astype(BF)
    got_om.wait()
    pan[1] = mm(gl[1], om[...])
    first(1, pan[1, :, cols(1 - core)])
    got_mate.wait_recv()
    pan[0] = mm(wf[1], om[...]) + mm(wf[2 * (1 - core)], om_mate[...])
    first(0, pan[0, :, cols(1 - core)])
    erows[...] = jnp.zeros_like(erows)
    for i in range(2):
        got_orders[i].wait_recv()
        erows[i : i + 1] = orders[i, 1:2, 0:128].astype(F32)
    ecols = erows[...].T
    for k, col in enumerate((ecols[0:K, 0:1], lcols[0:K, 1:2], ecols[0:K, 1:2])):
        at = (3 * core, 2, 3 * (1 - core))[k]
        wa[at] = mm_nt(onehot(col, 768).astype(BF), placed[:, k * 768 : (k + 1) * 768]).astype(BF)
    got_w.wait_recv()
    outward(0, mm(w_in[...], om[...]))

    def chain_send(ch, i):
        return pltpu.make_async_remote_copy(
            src_ref=hi.at[0, 2 * ch + i],
            dst_ref=rec.at[0, i],
            send_sem=ss.at[0, i],
            recv_sem=rs.at[0, i],
            device_id=partners[1],
            device_id_type=MESH,
        )

    def chain_start(ch, i):
        @pl.when(z0 == 1 - ch)
        def _():
            chain_send(ch, i).start()

    def tests_up(ch):
        own, far = ch * 2 + core, ch * 2 + 1 - core
        q = 2 * ch + 1
        top, low = split(pan[q, :, cols(core)])
        firsts[q].wait_recv()
        top_new, lo[q] = split(twice(op_g[own][:, :K], top, low) + mm(op_g[far][:, :K], r0[q]))
        hi[0, q] = top_new
        chain_start(ch, 1)
        return twice(op_h[own][:, :K], top, low) + mm(op_h[far][:, :K], r0[q])

    def rows_up(ch, coupled, own_rows, far_rows):
        own, far = ch * 2 + core, ch * 2 + 1 - core
        new = twice(op_s[own][:, :K], *split(own_rows)) + twice(op_s[far][:, :K], *split(far_rows)) - coupled
        top_new, lo[2 * ch] = split(new)
        hi[0, 2 * ch] = top_new
        chain_start(ch, 0)
        out[0, ch, :, cols(core)] = top_new
        arrivals.append(
            send(hi.at[0, 2 * ch], out.at[0, ch, :, cols(core)], os_s.at[0, ch], os_r.at[0, ch], partners[0])
        )

    arrivals = []
    coupled_fwd = tests_up(0)

    own_tests.wait()
    everyone = adj_in.at[pl.ds(0, 63)]
    trades = pltpu.make_async_remote_copy(
        src_ref=everyone,
        dst_ref=everyone,
        send_sem=a2a_s,
        recv_sem=a2a_r,
        device_id={"sub": right},
        device_id_type=MESH,
    )
    trades.wait_recv()
    adj[...] = adj_in[...].reshape(256, 768)
    outward(1, mm_nt(wa[0], adj[...]))
    inner = mm_nt(wa[1:4].reshape(3 * K, 768), adj[...])
    pan[3] = inner[0:K]
    pan[2] = inner[K : 2 * K]
    pan_far[...] = inner[2 * K :]
    first(3, pan[3, :, cols(1 - core)])
    first(4, pan[2, :, cols(1 - core)])
    first(2, pan_far[:, cols(1 - core)])
    firsts[0].wait_recv()
    outward_done(0)
    rows_up(
        0,
        coupled_fwd,
        pan[0, :, cols(core)] + d_r[0, core].astype(F32),
        r0[0].astype(F32) + d_r[0, 1 - core].astype(F32),
    )
    coupled_adj = tests_up(1)
    firsts[2].wait_recv()
    firsts[4].wait_recv()
    outward_done(1)
    rows_up(
        1,
        coupled_adj,
        pan[2, :, cols(core)] + r0[2].astype(F32) + d_r[1, core].astype(F32),
        pan_far[:, cols(core)] + r0[4].astype(F32) + d_r[1, 1 - core].astype(F32),
    )
    ways = [chain_send(0, 0), chain_send(0, 1)]
    started += ways
    f_top, o_top = hi[0, 2 * z0], hi[0, 2 * z0 + 1]
    f_low, o_low = lo[2 * z0], lo[2 * z0 + 1]
    peers = ({"sub": cross}, {"sub": zmate}, {"sub": mate})
    def publish(j, top=None):
        if top is not None:
            hi[j, 0] = top
        for k, who in enumerate(peers):
            arrivals.append(
                send(hi.at[j, 0], out.at[j, z0, :, cols(core)], os_s.at[j, k], os_r.at[j, k], who)
            )
        if top is not None:
            out[j, z0, :, cols(core)] = top

    last = LEVELS - 3
    for j in range(1, last + 1):
        base = (j * 2 + z0) * 2
        own, far = base + bits[j], base + 1 - bits[j]
        o_part = twice(op_g[own][:, :K], o_top, o_low)
        f_part = twice(op_s[own][:, :K], f_top, f_low) - twice(op_h[own][:, :K], o_top, o_low)
        ways[1].wait_recv()
        o_far = rec[j - 1, 1]
        nexts = [None, None]
        o_top, o_low = split(o_part + mm(op_g[far][:, :K], o_far))
        if j < last:
            hi[j, 1] = o_top
            nexts[1] = send(hi.at[j, 1], rec.at[j, 1], ss.at[j, 1], rs.at[j, 1], partners[j + 1])
        f_part = f_part - mm(op_h[far][:, :K], o_far)
        ways[0].wait_recv()
        f_top, f_low = split(f_part + mm(op_s[far][:, :K], rec[j - 1, 0]))
        if j < last:
            hi[j, 0] = f_top
            nexts[0] = send(hi.at[j, 0], rec.at[j, 0], ss.at[j, 0], rs.at[j, 0], partners[j + 1])
            out[j, z0, :, cols(core)] = f_top
            for due in {3: (1, 2), 4: (3, 4), 5: (5,)}.get(j, ()):
                publish(due)
        ways = nexts

    a = ((LEVELS - 2) * 2 + z0) * 2 + bits[LEVELS - 2]
    b = ((LEVELS - 1) * 2 + z0) * 2 + bits[LEVELS - 1]
    o_seven = twice(op_g[a][:, :K], o_top, o_low)
    h_eight = twice(op_h[b][:, :K], *split(o_seven))
    f_seven = twice(op_s[a][:, :K], f_top, f_low) - twice(op_h[a][:, :K], o_top, o_low)
    fin_s[1] = f_seven.astype(BF)
    f_eight = twice(op_s[b][:, :K], *split(f_seven)) - h_eight
    fin_s[0] = f_eight.astype(BF)
    got_eight = []
    for k, who in ((1, partners[9]), (2, partners[8]), (0, partners[7])):
        got_eight.append(send(fin_s.at[0], fin_r.at[k], fin_ss.at[k], fin_rs.at[k], who))
    got_seven = send(fin_s.at[1], fin_r.at[3], fin_ss.at[3], fin_rs.at[3], partners[7])
    publish(last, f_top)
    got_seven.wait_recv()
    publish(LEVELS - 2, (f_seven + fin_r[3].astype(F32)).astype(BF))
    for copy in got_eight:
        copy.wait_recv()
    for k in range(3):
        f_eight = f_eight + fin_r[k].astype(F32)
    publish(LEVELS - 1, f_eight.astype(BF))
    for copy in arrivals:
        copy.wait_recv()
    for copy in started:
        copy.wait_send()

    trades.wait_send()


def local(omega, adj_tests, near_tiles, tile_cols, leaf_perms, leaf_interp, node_perms, node_maps):
    dma = pltpu.SemaphoreType.DMA
    anywhere = pl.BlockSpec(memory_space=pl.ANY)
    ops = pltpu.VMEM((LEVELS * 4, K, 128), BF)
    return pl.pallas_call(
        kernel,
        out_shape=jax.ShapeDtypeStruct((LEVELS, 2, K, 256), BF),
        in_specs=[pl.BlockSpec(memory_space=pltpu.SMEM)] + [anywhere] * 7,
        out_specs=pl.BlockSpec(memory_space=pltpu.VMEM),
        scratch_shapes=[
            pltpu.VMEM((768, 256), BF),
            pltpu.VMEM((768, 256), BF),
            pltpu.VMEM((K, 768), BF),
            pltpu.VMEM((6, 12, 128, 128), BF),
            pltpu.VMEM((2, 768), jnp.int32),
            pltpu.VMEM((2, K, 672), BF),
            pltpu.VMEM((LEVELS, 2, 192), jnp.int32),
            pltpu.VMEM((LEVELS, 4, K, K), BF),
            pltpu.VMEM((24, 256), F32),
            pltpu.VMEM((8, 768), F32),
            pltpu.VMEM((8, 128), F32),
            pltpu.VMEM((2, 2, 768), jnp.int32),
            pltpu.VMEM((768, 2304), BF),
            pltpu.VMEM((3, K, 768), BF),
            pltpu.VMEM((4, K, 768), BF),
            pltpu.VMEM((2, K, 768), BF),
            ops,
            ops,
            ops,
            pltpu.VMEM((64, 4, 768), BF),
            pltpu.VMEM((256, 768), BF),
            pltpu.VMEM((4, K, 256), F32),
            pltpu.VMEM((K, 256), F32),
            pltpu.VMEM((2, 2, K, 128), BF),
            pltpu.VMEM((2, 2, K, 128), BF),
            pltpu.VMEM((5, K, 128), BF),
            pltpu.VMEM((5, K, 128), BF),
            pltpu.VMEM((LEVELS, 4, K, 128), BF),
            pltpu.VMEM((4, K, 128), BF),
            pltpu.VMEM((LEVELS - 1, 2, K, 128), BF),
            pltpu.VMEM((2, K, 128), BF),
            pltpu.VMEM((4, K, 128), BF),
            dma((7,)),
            dma,
            dma,
            dma((4,)),
            dma((4,)),
            dma((2, 2)),
            dma((2, 2)),
            dma((5,)),
            dma((5,)),
            dma((LEVELS, 2)),
            dma((LEVELS, 2)),
            dma((LEVELS, 3)),
            dma((LEVELS, 3)),
            dma((4,)),
            dma((4,)),
        ],
        compiler_params=pltpu.CompilerParams(
            collective_id=0, has_side_effects=True, vmem_limit_bytes=28 << 20
        ),
        name="window",
    )(
        *(
            pltpu.with_memory_space_constraint(x, pltpu.HBM)
            for x in (
                tile_cols,
                omega,
                adj_tests,
                near_tiles,
                leaf_perms,
                jnp.swapaxes(leaf_interp, 2, 3),
                node_perms,
                node_maps,
            )
        ),
    )[None]


def solution(mesh):
    placed = (
        P(("grp", "sub"), None),
        P("sub", "grp"),
        P(("grp", "sub"), None, None, None),
        P(("grp", "sub"), None),
        P(("grp", "sub"), None, None),
        P(("grp", "sub"), None, None, None),
        P(("grp", "sub"), None, None, None),
        P(("grp", "sub"), None, None, None, None),
    )
    return jax.shard_map(
        local,
        mesh=mesh,
        in_specs=placed,
        out_specs=P(("grp", "sub"), None, None, None, None),
        check_vma=False,
    )
```
